128 devices in a mesh: seq: 16 (over y_hi, z, core), head: 8 (over x, y_lo).
Axes of the slice: x: 4, y: 4 (y_hi: 2, y_lo: 2; y = y_hi * 2 + y_lo), z: 4, core: 2. Of those that a mesh axis runs over, the one named last changes fastest.
Arguments:
- attn_query: bfloat16 [32768, 5120], P('seq', 'head'), may hold values from -45 to 45
- attn_key: bfloat16 [32768, 5120], P('seq', 'head'), may hold values from -15 to 15
- attn_value: bfloat16 [32768, 5120], P('seq', 'head'), may hold values from -6 to 6
- fast_query: bfloat16 [32768, 5120], P('seq', 'head'), may hold values from -6 to 6
- fast_key: bfloat16 [32768, 5120], P('seq', 'head'), may hold values from -6 to 6
- fast_value: bfloat16 [32768, 5120], P('seq', 'head'), may hold values from -6 to 6
- rates: float32 [32768, 8], P('seq', 'head'), may hold values from 0.00015625 to 0.0015625
- fast_weights: float32 [8, 640, 3, 640], P('head'), may hold values from -0.25 to 0.25
- gain: float32 [8, 640], P('head'), may hold values from 0.5 to 1.5
Outputs:
- mixed: bfloat16 [32768, 5120], P('seq', 'head')
- final_weights: float32 [8, 640, 3, 640], P('head', 'seq')
The draws below stay inside these ranges and needn't reach their ends.
All inputs are finite; a program needn't handle non-finite values.
Results may differ from the reference program's by a relative error of at most 0.013.
Values may be sent and summed in bfloat16 or wider, within the bound.
No kernel may reach another device: no remote copies, remote signals or barrier semaphores. Data moves between devices by JAX's collectives and lax.ppermute only.
A program may use at most 192 MiB of HBM per device.

```python
import math
import jax
import jax.numpy as jnp
from jax import lax

DH = 640
FH = 640
AH = 128
WINDOW = 512
HEADS = 8
ATT_HEADS = 40
TOKENS = 32768


def attention_pair(seed_key):
    grid_shape = (TOKENS, ATT_HEADS * AH)
    base_key = jnp.clip(jax.random.normal(jax.random.fold_in(seed_key, 101), grid_shape, jnp.float32), -5.0, 5.0)
    base_query = jnp.clip(jax.random.normal(jax.random.fold_in(seed_key, 202), grid_shape, jnp.float32), -5.0, 5.0)
    return (base_query, base_key)


def draw_attn_query(key, part):
    return attention_pair(key)[0].astype(jnp.bfloat16)


def draw_attn_key(key, part):
    return attention_pair(key)[1].astype(jnp.bfloat16)


def level_of(key, dims, split, smallest, high):
    def one(axis_at, parts):
        steps = jax.random.uniform(jax.random.fold_in(jax.random.fold_in(key, 6), axis_at), (parts,), jnp.float32, smallest / len(split), high / len(split))
        return jnp.repeat(jnp.exp(steps), dims[axis_at] // parts).reshape((-1,) + (1,) * (len(dims) - axis_at - 1))

    level = one(*split[0])
    for cut in split[1:]:
        level = level * one(*cut)
    return level


def normal_values(own_key, dims, scale, reach, cuts=(), held_as=jnp.bfloat16):
    drawn = jax.random.normal(own_key, dims, jnp.float32) * scale
    if len(cuts) > 0:
        drawn = level_of(own_key, dims, cuts, -0.22, 0.18) * drawn
    return jnp.clip(drawn, min=-reach, max=reach).astype(held_as)


def setup_inputs(seed: int = 0) -> dict:
    arg_keys = jax.random.split(jax.random.key(seed), 10)
    attn_query = draw_attn_query(jax.random.fold_in(arg_keys[9], 71), 0)
    attn_key = draw_attn_key(jax.random.fold_in(arg_keys[9], 71), 0)
    attn_value = normal_values(arg_keys[2], (TOKENS, ATT_HEADS * AH), 1.0, 6.0, ((0, 16), (1, 8)))
    fast_query = normal_values(arg_keys[3], (TOKENS, HEADS * DH), 1.0, 6.0, ((0, 16), (1, 8)))
    fast_key = normal_values(arg_keys[4], (TOKENS, HEADS * DH), 1.0, 6.0, ((0, 16), (1, 8)))
    fast_value = normal_values(arg_keys[5], (TOKENS, HEADS * DH), 1.0, 6.0, ((0, 16), (1, 8)))
    rates = jnp.clip(jnp.exp(math.log(0.0015625) - 2.3025851 * jax.random.uniform(arg_keys[6], (TOKENS, HEADS), jnp.float32) ** level_of(arg_keys[6], (TOKENS, HEADS), ((0, 16), (1, 8)), -0.2, 0.2)), 0.00015625, 0.0015625)
    fast_weights = normal_values(arg_keys[7], (HEADS, FH, 3, DH), DH ** -0.5, 0.25, ((0, 8),), jnp.float32)
    gain = jnp.clip(1.0 + 0.1 * jax.random.normal(arg_keys[8], (HEADS, DH), jnp.float32), 0.5, 1.5)
    return dict(attn_query=attn_query, attn_key=attn_key, attn_value=attn_value, fast_query=fast_query, fast_key=fast_key, fast_value=fast_value, rates=rates, fast_weights=fast_weights, gain=gain)


EPSILON = 1e-06

def window_attention(queries, key_rows, value_rows):
    total_rows, columns = queries.shape
    head_count = columns // AH
    tile_rows = min(total_rows, 512)
    zero_rows = jnp.zeros((WINDOW, columns), queries.dtype)
    padded_keys = jnp.concatenate([zero_rows, key_rows], 0)
    padded_values = jnp.concatenate([zero_rows, value_rows], 0)

    def one_tile(tile_index):
        tile_start = tile_index * tile_rows
        query_tile = lax.dynamic_slice_in_dim(queries, tile_start, tile_rows, 0).astype(jnp.float32).reshape(tile_rows, head_count, AH)
        key_tile = lax.dynamic_slice_in_dim(padded_keys, tile_start, tile_rows + WINDOW, 0).astype(jnp.float32).reshape(tile_rows + WINDOW, head_count, AH)
        value_tile = lax.dynamic_slice_in_dim(padded_values, tile_start, tile_rows + WINDOW, 0).astype(jnp.float32).reshape(tile_rows + WINDOW, head_count, AH)
        scores = jnp.einsum('qhd,khd->hqk', query_tile, key_tile) * (1.0 / math.sqrt(AH))
        query_pos = tile_start + jnp.arange(tile_rows, dtype=jnp.int32)
        key_pos = tile_start - WINDOW + jnp.arange(tile_rows + WINDOW, dtype=jnp.int32)
        distance = query_pos[:, None] - key_pos[None, :]
        allowed = (distance >= 0) & (distance < WINDOW) & (key_pos[None, :] >= 0)
        scores = jnp.where(allowed[None], scores, -1e+30)
        row_max = lax.optimization_barrier(jnp.max(scores, axis=-1, keepdims=True))
        weights = jnp.exp(scores - row_max)
        row_total = lax.optimization_barrier(jnp.sum(weights, axis=-1, keepdims=True))
        probabilities = (weights / row_total).astype(jnp.bfloat16)
        result = jnp.einsum('hqk,khd->qhd', probabilities.astype(jnp.float32), value_tile)
        return result.reshape(tile_rows, columns)
    tiles = lax.map(one_tile, jnp.arange(total_rows // tile_rows, dtype=jnp.int32))
    return tiles.reshape(total_rows, columns)

def block_gradient(weights, key_rows, value_rows, rate_rows):
    gate_pre = jnp.dot(key_rows, weights[:, 0, :].T, preferred_element_type=jnp.float32)
    up_pre = jnp.dot(key_rows, weights[:, 1, :].T, preferred_element_type=jnp.float32)
    active = jax.nn.silu(gate_pre)
    hidden = (active * up_pre).astype(jnp.bfloat16)
    signal = (rate_rows * value_rows.astype(jnp.float32)).astype(jnp.bfloat16)
    back_grad = jnp.dot(signal, weights[:, 2, :].T, preferred_element_type=jnp.float32)
    sigmoid_gate = jax.nn.sigmoid(gate_pre)
    up_grad = (back_grad * active).astype(jnp.bfloat16)
    gate_grad = (back_grad * up_pre * sigmoid_gate * (1.0 + gate_pre * (1.0 - sigmoid_gate))).astype(jnp.bfloat16)
    gate_term = jnp.dot(gate_grad.T, key_rows, preferred_element_type=jnp.float32)
    up_term = jnp.dot(up_grad.T, key_rows, preferred_element_type=jnp.float32)
    down_term = jnp.dot(hidden.T, signal, preferred_element_type=jnp.float32)
    return jnp.stack([gate_term, up_term, down_term], axis=1)

def renormalize(previous, gradient):
    moved = previous + gradient
    norm_ratio = jnp.sqrt(lax.optimization_barrier(jnp.mean(previous * previous, axis=-1, keepdims=True)) + EPSILON) / jnp.sqrt(lax.optimization_barrier(jnp.mean(moved * moved, axis=-1, keepdims=True)) + EPSILON)
    return moved * norm_ratio

def fast_apply(weights, query_rows, gain_row):
    gate_pre = jnp.dot(query_rows, weights[:, 0, :].T, preferred_element_type=jnp.float32)
    up_pre = jnp.dot(query_rows, weights[:, 1, :].T, preferred_element_type=jnp.float32)
    hidden = (jax.nn.silu(gate_pre) * up_pre).astype(jnp.bfloat16)
    output = jnp.dot(hidden, weights[:, 2, :], preferred_element_type=jnp.float32)
    inverse_rms = lax.rsqrt(lax.optimization_barrier(jnp.mean(output * output, axis=-1, keepdims=True)) + EPSILON)
    return output * inverse_rms * gain_row

def reference(attn_query, attn_key, attn_value, fast_query, fast_key, fast_value, rates, fast_weights, gain):
    attended = window_attention(attn_query, attn_key, attn_value)
    half_rows = TOKENS // 2
    pieces = []
    finals = []
    for head_index in range(HEADS):
        low = head_index * DH
        head_queries = fast_query[:, low:low + DH]
        head_keys = fast_key[:, low:low + DH]
        head_values = fast_value[:, low:low + DH]
        head_rates = rates[:, head_index:head_index + 1]
        initial = fast_weights[head_index]
        first_cast = initial.astype(jnp.bfloat16)
        first_gradient = block_gradient(first_cast, head_keys[:half_rows], head_values[:half_rows], head_rates[:half_rows])
        middle = renormalize(initial, first_gradient)
        middle_cast = middle.astype(jnp.bfloat16)
        second_gradient = block_gradient(middle_cast, head_keys[half_rows:], head_values[half_rows:], head_rates[half_rows:])
        finals.append(renormalize(middle, second_gradient))
        early_out = fast_apply(first_cast, head_queries[:half_rows], gain[head_index])
        later_out = fast_apply(middle_cast, head_queries[half_rows:], gain[head_index])
        pieces.append(jnp.concatenate([early_out, later_out], 0))
    mixed = (attended + jnp.concatenate(pieces, 1)).astype(jnp.bfloat16)
    return (mixed, jnp.stack(finals))
```

```python
import math
from functools import partial

import jax
import jax.numpy as jnp
from jax import lax
from jax.experimental import pallas as pl
from jax.experimental.pallas import tpu as pltpu
from jax.sharding import PartitionSpec as P

AH = 128
WINDOW = 512
SUB = 256
EPSILON = 1e-06
F32 = jnp.float32
BF16 = jnp.bfloat16


def dot(a, b, contract):
    return lax.dot_general(a, b, (contract, ((), ())), preferred_element_type=F32)


NT = ((1,), (1,))
NN = ((1,), (0,))


def params(mib=56):
    return pltpu.CompilerParams(
        dimension_semantics=("arbitrary",), vmem_limit_bytes=mib << 20
    )


def attention_body(first, info_ref, q_ref, kp_ref, kc_ref, vp_ref, vc_ref, o_ref):
    heads = q_ref.shape[1] // AH
    scale = math.log2(math.e) / math.sqrt(AH)
    row = lax.broadcasted_iota(jnp.int32, (SUB, SUB), 0)
    col = lax.broadcasted_iota(jnp.int32, (SUB, SUB), 1)
    older = col > row
    ones = jnp.ones((SUB, AH), BF16)
    bias = jnp.where(info_ref[0] == 0, -1e30, 0.0).astype(F32) if first else None
    for h in range(heads):
        cols = slice(h * AH, (h + 1) * AH)
        keys = [kp_ref[:SUB, cols], kp_ref[SUB:, cols], kc_ref[:SUB, cols], kc_ref[SUB:, cols]]
        values = [
            jnp.concatenate([v, ones], 1)
            for v in (vp_ref[:SUB, cols], vp_ref[SUB:, cols], vc_ref[:SUB, cols], vc_ref[SUB:, cols])
        ]
        for strip in range(2):
            q = q_ref[strip * SUB : (strip + 1) * SUB, cols]
            old, mid, new = (dot(q, keys[strip + n], NT) for n in range(3))
            if first:
                old = old + bias
                if strip == 0:
                    mid = mid + bias
            edge = jnp.where(older, old, new)
            top = jnp.max(jnp.maximum(edge, mid), axis=1, keepdims=True)
            edge = jnp.exp2((edge - top) * scale)
            mid = jnp.exp2((mid - top) * scale).astype(BF16)
            old = jnp.where(older, edge, 0.0).astype(BF16)
            new = jnp.where(older, 0.0, edge).astype(BF16)
            out = (
                dot(old, values[strip], NN)
                + dot(mid, values[strip + 1], NN)
                + dot(new, values[strip + 2], NN)
            )
            o_ref[strip * SUB : (strip + 1) * SUB, cols] = out[:, :AH] / out[:, AH:]


def attention_first(info, q, k, v, halo_k, halo_v, partly):
    rows, width = q.shape
    tile = pl.BlockSpec((WINDOW, width), lambda i, s: (0, 0))
    kernel = partial(attention_body, True)

    def body(info_ref, q_ref, kp_ref, kc_ref, vp_ref, vc_ref, _, o_ref):
        kernel(info_ref, q_ref, kp_ref, kc_ref, vp_ref, vc_ref, o_ref)

    return pl.pallas_call(
        body,
        out_shape=jax.ShapeDtypeStruct((rows, width), F32),
        grid_spec=pltpu.PrefetchScalarGridSpec(
            num_scalar_prefetch=1,
            grid=(1,),
            in_specs=[tile, tile, tile, tile, tile, pl.BlockSpec(memory_space=pl.ANY)],
            out_specs=tile,
        ),
        input_output_aliases={6: 0},
        compiler_params=params(),
        name="attention_first",
    )(info, q, halo_k, k, halo_v, v, partly)


def attention_rest(info, q, k, v):
    rows, width = q.shape
    here = pl.BlockSpec((WINDOW, width), lambda i, s: (i + 1, 0))
    before = pl.BlockSpec((WINDOW, width), lambda i, s: (i, 0))
    return pl.pallas_call(
        partial(attention_body, False),
        out_shape=jax.ShapeDtypeStruct((rows, width), F32),
        grid_spec=pltpu.PrefetchScalarGridSpec(
            num_scalar_prefetch=1,
            grid=(rows // WINDOW - 1,),
            in_specs=[here, before, here, before, here],
            out_specs=here,
        ),
        compiler_params=params(),
        name="attention_rest",
    )(info, q, k, k, v, v)


SLOTS = 8


def gradient_step(w_ref, key_ref, value_ref, rate_ref, acc_ref, step):
    hidden_units = w_ref.shape[0] // 3
    keys = key_ref[...]
    values = value_ref[...]
    rate = rate_ref[...]
    part = hidden_units // 2
    for n in range(2):
        lo = n * part
        gate_pre = dot(w_ref[lo : lo + part], keys, NT)
        up_pre = dot(w_ref[hidden_units + lo : hidden_units + lo + part], keys, NT)
        back = dot(w_ref[2 * hidden_units + lo : 2 * hidden_units + lo + part], values, NT) * rate
        sig = 0.5 * jnp.tanh(0.5 * gate_pre) + 0.5
        active = gate_pre * sig
        hidden = (active * up_pre * rate).astype(BF16)
        up_grad = (back * active).astype(BF16)
        gate_grad = (back * up_pre * (sig + active * (1.0 - sig))).astype(BF16)
        for m, (left, right) in enumerate(((gate_grad, keys), (up_grad, keys), (hidden, values))):
            at = pl.ds(m * hidden_units + lo, part)
            term = dot(left, right, NN)

            @pl.when(step == 0)
            def _():
                acc_ref[at] = term

            @pl.when(step > 0)
            def _():
                acc_ref[at] += term


def write_pieces(acc_ref, mine_ref, theirs_ref):
    hidden_units = acc_ref.shape[0] // 3
    span = hidden_units // SLOTS
    for d in range(SLOTS // 2):
        for e, ref in enumerate((mine_ref, theirs_ref)):
            for m in range(3):
                at = m * hidden_units + span * (2 * d + e)
                ref[d, m * span : (m + 1) * span] = acc_ref[at : at + span].astype(BF16)


def first_body(info_ref, fw_ref, key_ref, value_ref, rate_ref, mine_ref, theirs_ref, w_ref, acc_ref):
    step = pl.program_id(0)
    hidden_units = fw_ref.shape[1]
    span = hidden_units // SLOTS
    half = span // 2
    z, c = info_ref[2], info_ref[3]

    @pl.when(info_ref[1] == 0)
    def _():
        @pl.when(step == 0)
        def _():
            for d in range(SLOTS // 2):
                for e in range(2):
                    owner = 2 * lax.rem(z + d, 4) + (c if e == 0 else 1 - c)
                    start = pl.multiple_of(owner * half, 8)
                    late = pl.multiple_of(owner * half + hidden_units // 2, 8)
                    for m in range(3):
                        rows = jnp.concatenate(
                            [fw_ref[m, pl.ds(start, half)], fw_ref[m, pl.ds(late, half)]], 0
                        )
                        at = m * hidden_units + span * (2 * d + e)
                        w_ref[at : at + span] = rows.astype(BF16)

        gradient_step(w_ref, key_ref, value_ref, rate_ref, acc_ref, step)

        @pl.when(step == pl.num_programs(0) - 1)
        def _():
            write_pieces(acc_ref, mine_ref, theirs_ref)


def second_body(info_ref, *refs):
    pieces, (old_ref, key_ref, value_ref, rate_ref, mine_ref, theirs_ref, w_ref, acc_ref) = (
        refs[:SLOTS],
        refs[SLOTS:],
    )
    step = pl.program_id(0)
    hidden_units = w_ref.shape[0] // 3
    span = hidden_units // SLOTS

    @pl.when(info_ref[1] == 0)
    def _():
        @pl.when(step == 0)
        def _():
            w_ref[...] = old_ref[...]

    @pl.when(info_ref[1] == 1)
    def _():
        @pl.when(step == 0)
        def _():
            for d in range(SLOTS // 2):
                for e in range(2):
                    ref = pieces[e * SLOTS // 2 + (-d) % (SLOTS // 2)]
                    for m in range(3):
                        at = m * hidden_units + span * (2 * d + e)
                        w_ref[at : at + span] = ref[m * span : (m + 1) * span]

        gradient_step(w_ref, key_ref, value_ref, rate_ref, acc_ref, step)

        @pl.when(step == pl.num_programs(0) - 1)
        def _():
            write_pieces(acc_ref, mine_ref, theirs_ref)


def gradient_call(body, name, info, weights, keys, values, rates, hidden_units, tile=512):
    rows, width = keys.shape
    span = hidden_units // SLOTS
    part = (SLOTS // 2, 3 * span, width)
    whole = lambda shape: pl.BlockSpec(
        shape, lambda i, s: (0,) * len(shape), pipeline_mode=pl.Buffered(1)
    )
    stream = pl.BlockSpec((tile, width), lambda i, s: (i, 0))
    return pl.pallas_call(
        body,
        out_shape=(
            jax.ShapeDtypeStruct(part, BF16),
            jax.ShapeDtypeStruct(part, BF16),
            jax.ShapeDtypeStruct((3 * hidden_units, width), BF16),
        ),
        grid_spec=pltpu.PrefetchScalarGridSpec(
            num_scalar_prefetch=1,
            grid=(rows // tile,),
            in_specs=[whole(w.shape) for w in weights]
            + [stream, stream, pl.BlockSpec((1, tile), lambda i, s: (0, i))],
            out_specs=[whole(part), whole(part), whole((3 * hidden_units, width))],
            scratch_shapes=[pltpu.VMEM((3 * hidden_units, width), F32)],
        ),
        compiler_params=params(),
        name=name,
    )(info, *weights, keys, values, rates)


def apply_body(q_ref, w_ref, gain_ref, att_ref, o_ref):
    hidden_units = w_ref.shape[0] // 3
    q = q_ref[...]
    gate_pre = dot(q, w_ref[:hidden_units], NT)
    up_pre = dot(q, w_ref[hidden_units : 2 * hidden_units], NT)
    sig = 0.5 * jnp.tanh(0.5 * gate_pre) + 0.5
    hidden = (gate_pre * sig * up_pre).astype(BF16)
    out = dot(hidden, w_ref[2 * hidden_units :], NN)
    inverse_rms = lax.rsqrt(jnp.mean(out * out, axis=-1, keepdims=True) + EPSILON)
    o_ref[...] = (att_ref[...] + out * inverse_rms * gain_ref[...]).astype(BF16)


def fast_apply(queries, weights, gain, attended, tile=512):
    rows, width = queries.shape
    stream = pl.BlockSpec((tile, width), lambda i: (i, 0))
    return pl.pallas_call(
        apply_body,
        out_shape=jax.ShapeDtypeStruct((rows, width), BF16),
        grid=(rows // tile,),
        in_specs=[
            stream,
            pl.BlockSpec(weights.shape, lambda i: (0, 0), pipeline_mode=pl.Buffered(1)),
            pl.BlockSpec((1, width), lambda i: (0, 0)),
            stream,
        ],
        out_specs=stream,
        compiler_params=params(),
        name="fast_apply",
    )(queries, weights, gain, attended)


def renormalize(previous, gradient):
    moved = previous + gradient
    size = jnp.mean(previous * previous, axis=-1, keepdims=True) + EPSILON
    moved_size = jnp.mean(moved * moved, axis=-1, keepdims=True) + EPSILON
    return moved * (jnp.sqrt(size) / jnp.sqrt(moved_size))


def total(mine_ref, other_ref, arrived):
    out = mine_ref[0].astype(F32) + other_ref[0].astype(F32)
    for ref in arrived:
        out = out + ref[...].astype(F32)
    return out


def middle_body(info_ref, mine_ref, other_ref, a_ref, b_ref, c_ref, w0_ref, w1_ref, cast_ref, m0_ref, m1_ref):
    gradient = total(mine_ref, other_ref, (a_ref, b_ref, c_ref))
    half = w0_ref.shape[1]
    for m in range(3):
        rows = []
        for h, (w_ref, m_ref) in enumerate(((w0_ref, m0_ref), (w1_ref, m1_ref))):
            at = (2 * m + h) * half
            new = renormalize(w_ref[m], gradient[at : at + half])
            m_ref[m] = new
            rows.append(new)
        cast_ref[2 * m * half : 2 * (m + 1) * half] = jnp.concatenate(rows, 0).astype(BF16)


def middle_call(info, mine, other, arrived, fast_weights):
    _, span3, width = mine.shape
    half = span3 // 6
    lead = pl.BlockSpec((1, span3, width), lambda i, s: (0, 0, 0))
    flat = pl.BlockSpec((span3, width), lambda i, s: (0, 0))
    owned = pl.BlockSpec((3, half, width), lambda i, s: (0, 0, 0))
    return pl.pallas_call(
        middle_body,
        out_shape=(
            jax.ShapeDtypeStruct((span3, width), BF16),
            jax.ShapeDtypeStruct((3, half, width), F32),
            jax.ShapeDtypeStruct((3, half, width), F32),
        ),
        grid_spec=pltpu.PrefetchScalarGridSpec(
            num_scalar_prefetch=1,
            grid=(1,),
            in_specs=[lead, lead, flat, flat, flat]
            + [
                pl.BlockSpec((3, half, width), lambda i, s: (0, 2 * s[2] + s[3], 0)),
                pl.BlockSpec((3, half, width), lambda i, s: (0, SLOTS + 2 * s[2] + s[3], 0)),
            ],
            out_specs=[flat, owned, owned],
        ),
        compiler_params=params(),
        name="middle_rows",
    )(info, mine, other, *arrived, fast_weights, fast_weights)


def second_sum_body(mine_ref, other_ref, a_ref, b_ref, c_ref, s0_ref, s1_ref):
    gradient = total(mine_ref, other_ref, (a_ref, b_ref, c_ref))
    half = s0_ref.shape[1]
    for m in range(3):
        at = 2 * m * half
        s0_ref[m] = gradient[at : at + half].astype(BF16)
        s1_ref[m] = gradient[at + half : at + 2 * half]


def second_sum(mine, other, arrived):
    _, span3, width = mine.shape
    half = span3 // 6
    lead = pl.BlockSpec((1, span3, width), lambda i: (0, 0, 0))
    flat = pl.BlockSpec((span3, width), lambda i: (0, 0))
    owned = pl.BlockSpec((3, half, width), lambda i: (0, 0, 0))
    return pl.pallas_call(
        second_sum_body,
        out_shape=(
            jax.ShapeDtypeStruct((3, half, width), BF16),
            jax.ShapeDtypeStruct((3, half, width), F32),
        ),
        grid=(1,),
        in_specs=[lead, lead, flat, flat, flat],
        out_specs=[owned, owned],
        compiler_params=params(),
        name="second_sum",
    )(mine, other, *arrived)


def final_body(info_ref, m0_ref, m1_ref, g0_ref, g1_ref, o_ref):
    @pl.when(info_ref[1] == 0)
    def _():
        for m in range(3):
            o_ref[m] = renormalize(m0_ref[m], g0_ref[m].astype(F32))

    @pl.when(info_ref[1] == 1)
    def _():
        for m in range(3):
            o_ref[m] = renormalize(m1_ref[m], g1_ref[m])


def final_call(info, m0, m1, g0, g1):
    whole = pl.BlockSpec(m0.shape, lambda i, s: (0, 0, 0))
    return pl.pallas_call(
        final_body,
        out_shape=jax.ShapeDtypeStruct(m0.shape, F32),
        grid_spec=pltpu.PrefetchScalarGridSpec(
            num_scalar_prefetch=1, grid=(1,), in_specs=[whole] * 4, out_specs=whole
        ),
        compiler_params=params(),
        name="final_rows",
    )(info, m0, m1, g0, g1)


def send(x, pairs):
    return lax.ppermute(x, "seq", pairs)


def along_z(block, d):
    return [
        (8 * block + 2 * z + c, 8 * block + 2 * ((z + d) % 4) + c) for z in range(4) for c in range(2)
    ]


def sibling(block):
    return [(8 * block + k, 8 * block + (k ^ 1)) for k in range(8)]


ACROSS = [(k, k + 8) for k in range(8)]
BACK = [(k + 8, k) for k in range(8)]


def reduce_pieces(block, mine, theirs):
    other = send(theirs, sibling(block))
    joined = [
        (mine[d].astype(F32) + other[d].astype(F32)).astype(BF16) for d in range(1, SLOTS // 2)
    ]
    arrived = [send(piece, along_z(block, d + 1)) for d, piece in enumerate(joined)]
    return other, arrived


def shards(
    attn_query, attn_key, attn_value, fast_query, fast_key, fast_value, rates, fast_weights, gain
):
    row_count, width = attn_query.shape
    seq = lax.axis_index("seq").astype(jnp.int32)
    block = seq // 8
    info = jnp.stack([seq, block, (seq % 8) // 2, seq % 2])
    initial = jnp.transpose(fast_weights[0], (1, 0, 2))
    hidden_units = initial.shape[1]
    rate_row = rates.reshape(1, row_count)

    count = lax.axis_size("seq")
    onward = [(i, i + 1) for i in range(count - 1)]
    halo_k = send(attn_key[row_count - WINDOW :], onward)
    halo_v = send(attn_value[row_count - WINDOW :], onward)

    mine, theirs, first_cast = gradient_call(
        first_body, "first_gradient", info, [initial], fast_key, fast_value, rate_row, hidden_units
    )
    other, arrived = reduce_pieces(0, mine, theirs)
    attended = attention_rest(info, attn_query, attn_key, attn_value)
    cast, middle_0, middle_1 = middle_call(info, mine, other, arrived, initial)

    own = send(cast, ACROSS)
    column = [own] + [send(own, along_z(1, d)) for d in range(1, SLOTS // 2)]
    beside = [send(piece, sibling(1)) for piece in column]
    middle_1 = send(middle_1, ACROSS)
    attended = attention_first(info, attn_query, attn_key, attn_value, halo_k, halo_v, attended)

    mine, theirs, weights = gradient_call(
        second_body,
        "second_gradient",
        info,
        column + beside + [first_cast],
        fast_key,
        fast_value,
        rate_row,
        hidden_units,
    )
    other, arrived = reduce_pieces(1, mine, theirs)
    mixed = fast_apply(fast_query, weights, gain, attended)
    sum_0, sum_1 = second_sum(mine, other, arrived)
    sum_0 = send(sum_0, BACK)
    final = final_call(info, middle_0, middle_1, sum_0, sum_1)
    return mixed, jnp.transpose(final, (1, 0, 2))[None]


def solution(mesh):
    in_specs = (
        P("seq", "head"),
        P("seq", "head"),
        P("seq", "head"),
        P("seq", "head"),
        P("seq", "head"),
        P("seq", "head"),
        P("seq", "head"),
        P("head", None, None, None),
        P("head", None),
    )
    out_specs = (P("seq", "head"), P("head", "seq", None, None))
    return jax.shard_map(shards, mesh=mesh, in_specs=in_specs, out_specs=out_specs, check_vma=False)
```

```python
import math
from functools import partial

import jax
import jax.numpy as jnp
from jax import lax
from jax.experimental import pallas as pl
from jax.experimental.pallas import tpu as pltpu
from jax.sharding import PartitionSpec as P

AH = 128
WINDOW = 512
SUB = 256
EPSILON = 1e-06
F32 = jnp.float32
BF16 = jnp.bfloat16


def dot(a, b, contract):
    return lax.dot_general(a, b, (contract, ((), ())), preferred_element_type=F32)


NT = ((1,), (1,))
NN = ((1,), (0,))


def params(mib=40):
    return pltpu.CompilerParams(
        dimension_semantics=("arbitrary",), vmem_limit_bytes=mib << 20
    )


def attention_body(first, info_ref, q_ref, kp_ref, kc_ref, vp_ref, vc_ref, o_ref):
    heads = q_ref.shape[1] // AH
    scale = math.log2(math.e) / math.sqrt(AH)
    row = lax.broadcasted_iota(jnp.int32, (SUB, SUB), 0)
    col = lax.broadcasted_iota(jnp.int32, (SUB, SUB), 1)
    older = col > row
    ones = jnp.ones((SUB, AH), BF16)
    bias = jnp.where(info_ref[0] == 0, -1e30, 0.0).astype(F32) if first else None
    for h in range(heads):
        cols = slice(h * AH, (h + 1) * AH)
        keys = [kp_ref[:SUB, cols], kp_ref[SUB:, cols], kc_ref[:SUB, cols], kc_ref[SUB:, cols]]
        values = [
            jnp.concatenate([v, ones], 1)
            for v in (vp_ref[:SUB, cols], vp_ref[SUB:, cols], vc_ref[:SUB, cols], vc_ref[SUB:, cols])
        ]
        for strip in range(2):
            q = q_ref[strip * SUB : (strip + 1) * SUB, cols]
            old, mid, new = (dot(q, keys[strip + n], NT) for n in range(3))
            if first:
                old = old + bias
                if strip == 0:
                    mid = mid + bias
            edge = jnp.where(older, old, new)
            top = jnp.max(jnp.maximum(edge, mid), axis=1, keepdims=True)
            edge = jnp.exp2((edge - top) * scale)
            mid = jnp.exp2((mid - top) * scale).astype(BF16)
            old = jnp.where(older, edge, 0.0).astype(BF16)
            new = jnp.where(older, 0.0, edge).astype(BF16)
            out = (
                dot(old, values[strip], NN)
                + dot(mid, values[strip + 1], NN)
                + dot(new, values[strip + 2], NN)
            )
            o_ref[strip * SUB : (strip + 1) * SUB, cols] = out[:, :AH] / out[:, AH:]


def attention_first(info, q, k, v, halo_k, halo_v, partly):
    rows, width = q.shape
    tile = pl.BlockSpec((WINDOW, width), lambda i, s: (0, 0))

    def body(info_ref, q_ref, kp_ref, kc_ref, vp_ref, vc_ref, _, o_ref):
        attention_body(True, info_ref, q_ref, kp_ref, kc_ref, vp_ref, vc_ref, o_ref)

    return pl.pallas_call(
        body,
        out_shape=jax.ShapeDtypeStruct((rows, width), F32),
        grid_spec=pltpu.PrefetchScalarGridSpec(
            num_scalar_prefetch=1,
            grid=(1,),
            in_specs=[tile] * 5 + [pl.BlockSpec(memory_space=pl.ANY)],
            out_specs=tile,
        ),
        input_output_aliases={6: 0},
        compiler_params=params(),
        name="attention_first",
    )(info, q, halo_k, k, halo_v, v, partly)


def attention_rest(info, q, k, v, block, partly=None):
    rows, width = q.shape

    def at(offset):
        return pl.BlockSpec(
            (WINDOW, width), lambda i, s: (jnp.where(s[1] == block, i, 0) + offset, 0)
        )

    def body(info_ref, q_ref, kp_ref, kc_ref, vp_ref, vc_ref, *rest):
        @pl.when(info_ref[1] == block)
        def _():
            attention_body(False, info_ref, q_ref, kp_ref, kc_ref, vp_ref, vc_ref, rest[-1])

        if partly is not None:

            @pl.when(info_ref[1] != block)
            def _():
                rest[-1][...] = rest[0][...]

    kept = [] if partly is None else [partly]
    return pl.pallas_call(
        body,
        out_shape=jax.ShapeDtypeStruct((rows, width), F32),
        grid_spec=pltpu.PrefetchScalarGridSpec(
            num_scalar_prefetch=1,
            grid=(rows // WINDOW - 1,),
            in_specs=[at(1), at(0), at(1), at(0), at(1)]
            + [pl.BlockSpec((WINDOW, width), lambda i, s: (1, 0)) for _ in kept],
            out_specs=at(1),
        ),
        input_output_aliases={6: 0} if kept else {},
        compiler_params=params(),
        name=f"attention_rest_{block}",
    )(info, q, k, k, v, v, *kept)


SLOTS = 8
RING = 4


class Chunk:
    def __init__(self, name, spans):
        self.name = name
        self.spans = spans
        self.span = sum(n for _, _, n in spans)
        self.rows = SLOTS * self.span


EARLY = Chunk("early", ((0, 0, 40), (1, 0, 8)))
LATE = Chunk("late", ((1, 8, 32),))
CHUNKS = (EARLY, LATE)


def factors(chunk, base, w_ref, keys_ref, values_ref, rate_ref, x_ref, at):
    n = chunk.rows
    keys = keys_ref[at]
    values = values_ref[at]
    rate = rate_ref[:, at]
    gate_pre = dot(w_ref[:n], keys, NT)
    up_pre = dot(w_ref[n : 2 * n], keys, NT)
    back = dot(w_ref[2 * n :], values, NT) * rate
    sig = 0.5 * jnp.tanh(0.5 * gate_pre) + 0.5
    active = gate_pre * sig
    x_ref[0, base : base + n, at] = (back * up_pre * (sig + active * (1.0 - sig))).astype(BF16)
    x_ref[1, base : base + n, at] = (back * active).astype(BF16)
    x_ref[2, base : base + n, at] = (active * up_pre * rate).astype(BF16)


TILE = 512


class Tokens:
    def __init__(self, key_hbm, value_hbm, keys_ref, values_ref, sems):
        self.pairs = ((key_hbm, keys_ref), (value_hbm, values_ref))
        self.sems = sems
        self.count = keys_ref.shape[0] // TILE

    def at(self, t):
        return pl.ds(pl.multiple_of(t * TILE, TILE), TILE)

    def copies(self, t):
        return [
            pltpu.make_async_copy(hbm.at[self.at(t)], ref.at[self.at(t)], self.sems.at[n, t])
            for n, (hbm, ref) in enumerate(self.pairs)
        ]

    def start(self, t):
        for copy in self.copies(t):
            copy.start()

    def wait(self, t):
        for copy in self.copies(t):
            copy.wait()


def contract(x_ref, keys_ref, values_ref, outs):
    for m in range(3):
        right = (values_ref if m == 2 else keys_ref)[...]
        term = dot(x_ref[m], right, NN)
        base = 0
        for chunk, (mine_ref, theirs_ref) in zip(CHUNKS, outs):
            span = chunk.span
            for d in range(RING):
                for e, ref in enumerate((mine_ref, theirs_ref)):
                    at = base + span * (2 * d + e)
                    ref[d, m * span : (m + 1) * span] = term[at : at + span].astype(BF16)
            base += chunk.rows


def row_copies(chunk, info_ref, fw_hbm, rows_ref, sems):
    half = fw_hbm.shape[1] // 2
    owned = half // SLOTS
    z, c = info_ref[2], info_ref[3]
    copies = []
    for d in range(RING):
        for e in range(2):
            owner = 2 * lax.rem(z + d, RING) + (c if e == 0 else 1 - c)
            at = (2 * d + e) * chunk.span
            for h, lo, n in chunk.spans:
                start = pl.multiple_of(owner * owned + h * half + lo, 8)
                copies.append(
                    pltpu.make_async_copy(
                        fw_hbm.at[:, pl.ds(start, n)],
                        rows_ref.at[:, pl.ds(at, n)],
                        sems.at[len(copies)],
                    )
                )
                at += n
    return copies


def fill_gathered(chunk, base, sources, w_ref):
    for d in range(RING):
        for e in range(2):
            from_there = (-d) % RING
            ref = sources[RING].at[from_there] if e else sources[from_there]
            for m in range(3):
                at = (m * SLOTS + 2 * d + e) * chunk.span
                here = base + m * chunk.span
                w_ref[at : at + chunk.span] = ref[here : here + chunk.span]


HERE = pl.BlockSpec(memory_space=pltpu.VMEM)
ANYWHERE = pl.BlockSpec(memory_space=pl.ANY)


SPLIT = 3 * EARLY.span
PIECE = SPLIT + 3 * LATE.span


def gradient_shapes(rows, width, chunked):
    heights = (SPLIT, PIECE - SPLIT) if chunked else (PIECE,)
    pieces = [
        jax.ShapeDtypeStruct((RING, height, width), BF16) for height in heights for _ in range(2)
    ]
    scratch = [pltpu.VMEM((3 * chunk.rows, width), BF16) for chunk in CHUNKS] + [
        pltpu.VMEM((3, sum(chunk.rows for chunk in CHUNKS), rows), BF16),
        pltpu.VMEM((rows, width), BF16),
        pltpu.VMEM((rows, width), BF16),
        pltpu.SemaphoreType.DMA((2,)),
        pltpu.SemaphoreType.DMA((2, rows // TILE)),
    ]
    return pieces, scratch


def gradient_first(info, initial, keys, values, rates):
    rows, width = keys.shape
    pieces, scratch = gradient_shapes(rows, width, False)
    weights = [jax.ShapeDtypeStruct((3 * chunk.rows, width), BF16) for chunk in CHUNKS]

    def body(info_ref, fw_hbm, key_hbm, value_hbm, rate_ref, mine, theirs, *refs):
        outs, held, refs = refs[:2], refs[2:4], refs[4:]
        x_ref, ks_ref, vs_ref, w_sems, t_sems, *refs = refs
        raw, row_sems = refs[:2], refs[2:]

        @pl.when(info_ref[1] == 0)
        def _():
            tokens = Tokens(key_hbm, value_hbm, ks_ref, vs_ref, t_sems)
            fetches = [
                row_copies(chunk, info_ref, fw_hbm, ref, sems)
                for chunk, ref, sems in zip(CHUNKS, raw, row_sems)
            ]
            saves = [pltpu.make_async_copy(held[i], outs[i], w_sems.at[i]) for i in range(2)]

            def part(i, t):
                base = i * EARLY.rows
                factors(CHUNKS[i], base, held[i], ks_ref, vs_ref, rate_ref, x_ref, tokens.at(t))

            for copy in fetches[0]:
                copy.start()
            tokens.start(0)
            for i, chunk in enumerate(CHUNKS):
                for copy in fetches[i]:
                    copy.wait()
                if i == 0:
                    for copy in fetches[1]:
                        copy.start()
                    tokens.start(1)
                for m in range(3):
                    held[i][m * chunk.rows : (m + 1) * chunk.rows] = raw[i][m].astype(BF16)
                if i == 0:
                    tokens.wait(0)
                part(i, 0)

            def one_tile(t, carry):
                @pl.when(t + 1 < tokens.count)
                def _():
                    tokens.start(t + 1)

                tokens.wait(t)
                part(0, t)
                part(1, t)
                return carry

            lax.fori_loop(1, tokens.count, one_tile, 0)
            for save in saves:
                save.start()
            halves = [
                [ref.at[:, at] for ref in (mine, theirs)]
                for at in (slice(0, SPLIT), slice(SPLIT, PIECE))
            ]
            contract(x_ref, ks_ref, vs_ref, halves)
            for save in saves:
                save.wait()

    return pl.pallas_call(
        body,
        out_shape=pieces + weights,
        grid_spec=pltpu.PrefetchScalarGridSpec(
            num_scalar_prefetch=1,
            grid=(1,),
            in_specs=[ANYWHERE] * 3 + [pl.BlockSpec(rates.shape, lambda i, s: (0, 0))],
            out_specs=[HERE] * 2 + [ANYWHERE] * 2,
            scratch_shapes=scratch
            + [pltpu.VMEM((3, chunk.rows, width), F32) for chunk in CHUNKS]
            + [pltpu.SemaphoreType.DMA((SLOTS * len(chunk.spans),)) for chunk in CHUNKS],
        ),
        compiler_params=params(),
        name="gradient_first",
    )(info, initial, keys, values, rates)


def gradient_second(info, gathered, keys, values, rates, kept):
    rows, width = keys.shape
    pieces, scratch = gradient_shapes(rows, width, True)
    count = RING + 1

    def body(info_ref, *refs):
        sources, refs = refs[:count], refs[count:]
        key_hbm, value_hbm, rate_ref, _, _, ma, ta, mb, tb, *refs = refs
        outs, held, refs = refs[:2], refs[2:4], refs[4:]
        x_ref, ks_ref, vs_ref, w_sems, t_sems = refs

        @pl.when(info_ref[1] == 1)
        def _():
            tokens = Tokens(key_hbm, value_hbm, ks_ref, vs_ref, t_sems)
            tokens.start(0)
            saves = [pltpu.make_async_copy(held[i], outs[i], w_sems.at[i]) for i in range(2)]
            for i, chunk in enumerate(CHUNKS):
                fill_gathered(chunk, i * SPLIT, sources, held[i])

            def one_tile(t, carry):
                @pl.when(t + 1 < tokens.count)
                def _():
                    tokens.start(t + 1)

                tokens.wait(t)
                for i, chunk in enumerate(CHUNKS):
                    base = i * EARLY.rows
                    factors(chunk, base, held[i], ks_ref, vs_ref, rate_ref, x_ref, tokens.at(t))
                return carry

            lax.fori_loop(0, tokens.count, one_tile, 0)
            for save in saves:
                save.start()
            contract(x_ref, ks_ref, vs_ref, ((ma, ta), (mb, tb)))
            for save in saves:
                save.wait()

    return pl.pallas_call(
        body,
        out_shape=pieces + [jax.ShapeDtypeStruct(w.shape, BF16) for w in kept],
        grid_spec=pltpu.PrefetchScalarGridSpec(
            num_scalar_prefetch=1,
            grid=(1,),
            in_specs=[HERE] * count
            + [ANYWHERE] * 2
            + [pl.BlockSpec(rates.shape, lambda i, s: (0, 0))]
            + [ANYWHERE] * 2,
            out_specs=[HERE] * 4 + [ANYWHERE] * 2,
            scratch_shapes=scratch,
        ),
        input_output_aliases={count + 4: 4, count + 5: 5},
        compiler_params=params(),
        name="gradient_second",
    )(info, *gathered, keys, values, rates, *kept)


def partial_output(q, w_ref):
    n = w_ref.shape[0] // 3
    gate_pre = dot(q, w_ref[:n], NT)
    up_pre = dot(q, w_ref[n : 2 * n], NT)
    sig = 0.5 * jnp.tanh(0.5 * gate_pre) + 0.5
    return dot((gate_pre * sig * up_pre).astype(BF16), w_ref[2 * n :], NN)


def fast_apply(info, queries, weights, gain, attended, tiles, partly=None, tile=512):
    rows, width = queries.shape
    stream = pl.BlockSpec((tile, width), lambda i, s: (i + tiles[0], 0))
    kept = [] if partly is None else [partly]

    def body(info_ref, q_ref, early_ref, late_ref, gain_ref, att_ref, *rest):
        q = q_ref[...]
        out = partial_output(q, early_ref) + partial_output(q, late_ref)
        inverse_rms = lax.rsqrt(jnp.mean(out * out, axis=-1, keepdims=True) + EPSILON)
        rest[-1][...] = (att_ref[...] + out * inverse_rms * gain_ref[...]).astype(BF16)

    return pl.pallas_call(
        body,
        out_shape=jax.ShapeDtypeStruct((rows, width), BF16),
        grid_spec=pltpu.PrefetchScalarGridSpec(
            num_scalar_prefetch=1,
            grid=(tiles[1] - tiles[0],),
            in_specs=[stream]
            + [
                pl.BlockSpec(w.shape, lambda i, s: (0, 0), pipeline_mode=pl.Buffered(1))
                for w in weights
            ]
            + [pl.BlockSpec((1, width), lambda i, s: (0, 0)), stream]
            + [ANYWHERE for _ in kept],
            out_specs=stream,
        ),
        input_output_aliases={6: 0} if kept else {},
        compiler_params=params(32),
        name=f"fast_apply_{tiles[0]}",
    )(info, queries, *weights, gain, attended, *kept)


def renormalize(previous, gradient):
    moved = previous + gradient
    size = jnp.mean(previous * previous, axis=-1, keepdims=True) + EPSILON
    moved_size = jnp.mean(moved * moved, axis=-1, keepdims=True) + EPSILON
    return moved * (jnp.sqrt(size) / jnp.sqrt(moved_size))


def total(mine_ref, other_ref, *arrived):
    out = mine_ref[0].astype(F32) + other_ref[0].astype(F32)
    for ref in arrived:
        out = out + ref[...].astype(F32)
    return out


def middle_call(info, mine, other, arrived, fast_weights):
    _, height, width = mine.shape
    owned = fast_weights.shape[1] // (2 * SLOTS)

    def half(h):
        return pl.BlockSpec(
            (3, owned, width), lambda i, s: (0, h * SLOTS + 2 * s[2] + s[3], 0)
        )

    def body(info_ref, mine_ref, other_ref, a_ref, b_ref, c_ref, w0_ref, w1_ref, cast_ref, keep_ref):
        gradient = total(mine_ref, other_ref, a_ref, b_ref, c_ref)
        base = 0
        for chunk in CHUNKS:
            for m in range(3):
                old = [(w0_ref, w1_ref)[h][m, lo : lo + n] for h, lo, n in chunk.spans]
                here = slice(base, base + chunk.span)
                new = renormalize(jnp.concatenate(old, 0), gradient[here])
                cast_ref[here] = new.astype(BF16)
                if chunk is EARLY:
                    keep_ref[m] = new[:owned]
                base += chunk.span

    return pl.pallas_call(
        body,
        out_shape=(
            jax.ShapeDtypeStruct((height, width), BF16),
            jax.ShapeDtypeStruct((3, owned, width), F32),
        ),
        grid_spec=pltpu.PrefetchScalarGridSpec(
            num_scalar_prefetch=1,
            grid=(1,),
            in_specs=[HERE] * 5 + [half(0), half(1)],
            out_specs=[HERE] * 2,
        ),
        compiler_params=params(16),
        name="middle_rows",
    )(info, mine, other, *arrived, fast_weights, fast_weights)


def sum_body(mine_ref, other_ref, a_ref, b_ref, c_ref, near_ref, far_ref):
    gradient = total(mine_ref, other_ref, a_ref, b_ref, c_ref)
    owned, rest = near_ref.shape[1], far_ref.shape[1]
    for m in range(3):
        at = m * (owned + rest)
        near_ref[m] = gradient[at : at + owned].astype(BF16)
        far_ref[m] = gradient[at + owned : at + owned + rest]


def sum_call(mine, other, arrived):
    _, span3, width = mine.shape
    owned = EARLY.spans[0][2]
    return pl.pallas_call(
        sum_body,
        out_shape=(
            jax.ShapeDtypeStruct((3, owned, width), BF16),
            jax.ShapeDtypeStruct((3, span3 // 3 - owned, width), F32),
        ),
        in_specs=[HERE] * 5,
        out_specs=[HERE] * 2,
        compiler_params=pltpu.CompilerParams(vmem_limit_bytes=16 << 20),
        name="second_sum",
    )(mine, other, *arrived)


def final_far(info, mine, other, arrived, cast, far):
    shape = (3, EARLY.spans[0][2], cast.shape[1])

    def body(info_ref, mine_ref, other_ref, a_ref, b_ref, c_ref, cast_ref, far_ref, o_ref):
        rest = far_ref.shape[1]
        owned = EARLY.span - rest

        @pl.when(info_ref[1] == 1)
        def _():
            gradient = total(mine_ref, other_ref, a_ref, b_ref, c_ref)
            for m in range(3):
                at = m * EARLY.span
                early = cast_ref[at : at + EARLY.span].astype(F32)[owned:]
                o_ref[m, :rest] = renormalize(early, far_ref[m])
                at = m * LATE.span
                late = cast_ref[SPLIT + at : SPLIT + at + LATE.span].astype(F32)
                o_ref[m, rest:] = renormalize(late, gradient[at : at + LATE.span])

    return pl.pallas_call(
        body,
        out_shape=jax.ShapeDtypeStruct(shape, F32),
        grid_spec=pltpu.PrefetchScalarGridSpec(
            num_scalar_prefetch=1, grid=(1,), in_specs=[HERE] * 7, out_specs=HERE
        ),
        compiler_params=params(16),
        name="final_far",
    )(info, mine, other, *arrived, cast, far)


def final_near(info, middle, near, far_rows):
    def body(info_ref, middle_ref, near_ref, far_ref, o_ref):
        @pl.when(info_ref[1] == 0)
        def _():
            for m in range(3):
                o_ref[m] = renormalize(middle_ref[m], near_ref[m].astype(F32))

        @pl.when(info_ref[1] == 1)
        def _():
            o_ref[...] = far_ref[...]

    return pl.pallas_call(
        body,
        out_shape=jax.ShapeDtypeStruct(middle.shape, F32),
        grid_spec=pltpu.PrefetchScalarGridSpec(
            num_scalar_prefetch=1, grid=(1,), in_specs=[HERE] * 3, out_specs=HERE
        ),
        compiler_params=params(16),
        name="final_near",
    )(info, middle, near, far_rows)


def send(x, pairs):
    return lax.ppermute(x, "seq", pairs)


def along_z(d):
    return [
        (8 * b + 2 * z + c, 8 * b + 2 * ((z + d) % RING) + c)
        for b in range(2)
        for z in range(RING)
        for c in range(2)
    ]


SIBLING = [(k, k ^ 1) for k in range(16)]
ACROSS = [(k, k + 8) for k in range(8)]
BACK = [(k + 8, k) for k in range(8)]


def in_hbm(x):
    return pltpu.with_memory_space_constraint(x, pltpu.HBM)


def after(x, *others):
    return lax.optimization_barrier((x, *others))[0]


def joined(mine, other):
    return [
        (mine[d].astype(F32) + other[d].astype(F32)).astype(BF16) for d in range(1, RING)
    ]


def around(pieces):
    return [send(piece, along_z(d + 1)) for d, piece in enumerate(pieces)]


def shards(
    attn_query, attn_key, attn_value, fast_query, fast_key, fast_value, rates, fast_weights, gain
):
    row_count, width = attn_query.shape
    seq = lax.axis_index("seq").astype(jnp.int32)
    info = jnp.stack([seq, seq // 8, (seq % 8) // 2, seq % 2])
    initial = in_hbm(jnp.transpose(fast_weights[0], (1, 0, 2)))
    tokens = (in_hbm(fast_key), in_hbm(fast_value), in_hbm(rates.reshape(1, row_count)))
    attn = tuple(in_hbm(x) for x in (attn_query, attn_key, attn_value))

    onward = [(i, (i + 1) % 16) for i in range(16)]
    tails = [x[row_count - WINDOW :] for x in (attn_key, attn_value)]

    mine, theirs, *weights = gradient_first(after(info, *tails), initial, *tokens)
    halo = [send(tail, onward) for tail in tails]
    other = send(after(theirs, *halo), SIBLING)
    parts = joined(mine, other)
    ring = around(parts)
    attended = attention_rest(after(info, *parts), *attn, 1)
    cast, middle = middle_call(after(info, attended), mine, other, ring, initial)
    own = send(cast, ACROSS)
    attended = attention_rest(after(info, cast), *attn, 0, attended)

    own = after(own, attended)
    ring = around([own] * (RING - 1))
    attended = attention_first(after(info, own), *attn, *halo, attended)
    column = [own] + [after(piece, attended) for piece in ring]
    beside = send(jnp.stack(column), SIBLING)
    mine_a, theirs_a, mine_b, theirs_b, *weights = gradient_second(
        info, [*column, beside], *tokens, weights
    )
    other_a = send(theirs_a, SIBLING)
    other_b = send(theirs_b, SIBLING)
    part_a = joined(mine_a, other_a)
    ring_a = around(part_a)
    part_b = joined(after(mine_b, *part_a), other_b)
    apply = partial(fast_apply, queries=fast_query, weights=weights, gain=gain, attended=attended)
    mixed = apply(after(info, *part_b), tiles=(0, 3))
    near, far = sum_call(after(mine_a, mixed), other_a, ring_a)
    near = send(near, BACK)
    ring_b = around(part_b)
    mixed = apply(after(info, far), tiles=(3, 4), partly=mixed)
    far_rows = final_far(after(info, mixed), mine_b, other_b, ring_b, own, far)
    final = final_near(info, middle, near, far_rows)
    return mixed, jnp.transpose(final, (1, 0, 2))[None]


def solution(mesh):
    in_specs = (
        P("seq", "head"),
        P("seq", "head"),
        P("seq", "head"),
        P("seq", "head"),
        P("seq", "head"),
        P("seq", "head"),
        P("seq", "head"),
        P("head", None, None, None),
        P("head", None),
    )
    out_specs = (P("seq", "head"), P("head", "seq", None, None))
    return jax.shard_map(shards, mesh=mesh, in_specs=in_specs, out_specs=out_specs, check_vma=False)
```

```python
import math
from functools import partial

import jax
import jax.numpy as jnp
from jax import lax
from jax.experimental import pallas as pl
from jax.experimental.pallas import tpu as pltpu
from jax.sharding import PartitionSpec as P

AH = 128
WINDOW = 512
SUB = 256
EPSILON = 1e-06
F32 = jnp.float32
BF16 = jnp.bfloat16


def dot(a, b, contract):
    return lax.dot_general(a, b, (contract, ((), ())), preferred_element_type=F32)


NT = ((1,), (1,))
NN = ((1,), (0,))


def params(mib=40):
    return pltpu.CompilerParams(
        dimension_semantics=("arbitrary",), vmem_limit_bytes=mib << 20
    )


def attention_body(first, info_ref, q_ref, kp_ref, kc_ref, vp_ref, vc_ref, o_ref):
    heads = q_ref.shape[1] // AH
    scale = math.log2(math.e) / math.sqrt(AH)
    row = lax.broadcasted_iota(jnp.int32, (SUB, SUB), 0)
    col = lax.broadcasted_iota(jnp.int32, (SUB, SUB), 1)
    older = col > row
    ones = jnp.ones((SUB, AH), BF16)
    bias = jnp.where(info_ref[0] == 0, -1e30, 0.0).astype(F32) if first else None
    for h in range(heads):
        cols = slice(h * AH, (h + 1) * AH)
        keys = [kp_ref[:SUB, cols], kp_ref[SUB:, cols], kc_ref[:SUB, cols], kc_ref[SUB:, cols]]
        values = [
            jnp.concatenate([v, ones], 1)
            for v in (vp_ref[:SUB, cols], vp_ref[SUB:, cols], vc_ref[:SUB, cols], vc_ref[SUB:, cols])
        ]
        for strip in range(2):
            q = q_ref[strip * SUB : (strip + 1) * SUB, cols]
            old, mid, new = (dot(q, keys[strip + n], NT) for n in range(3))
            if first:
                old = old + bias
                if strip == 0:
                    mid = mid + bias
            edge = jnp.where(older, old, new)
            top = jnp.max(jnp.maximum(edge, mid), axis=1, keepdims=True)
            edge = jnp.exp2((edge - top) * scale)
            mid = jnp.exp2((mid - top) * scale).astype(BF16)
            old = jnp.where(older, edge, 0.0).astype(BF16)
            new = jnp.where(older, 0.0, edge).astype(BF16)
            out = (
                dot(old, values[strip], NN)
                + dot(mid, values[strip + 1], NN)
                + dot(new, values[strip + 2], NN)
            )
            o_ref[strip * SUB : (strip + 1) * SUB, cols] = out[:, :AH] / out[:, AH:]


def attention_first(info, q, k, v, halo, partly):
    rows, width = q.shape
    tile = pl.BlockSpec((WINDOW, width), lambda i, s: (0, 0))

    def past(n):
        return pl.BlockSpec((None, WINDOW, width), lambda i, s: (n, 0, 0))

    def body(info_ref, q_ref, kp_ref, kc_ref, vp_ref, vc_ref, _, o_ref):
        attention_body(True, info_ref, q_ref, kp_ref, kc_ref, vp_ref, vc_ref, o_ref)

    return pl.pallas_call(
        body,
        out_shape=jax.ShapeDtypeStruct((rows, width), F32),
        grid_spec=pltpu.PrefetchScalarGridSpec(
            num_scalar_prefetch=1,
            grid=(1,),
            in_specs=[tile, past(0), tile, past(1), tile, pl.BlockSpec(memory_space=pl.ANY)],
            out_specs=tile,
        ),
        input_output_aliases={6: 0},
        compiler_params=params(),
        name="attention_first",
    )(info, q, halo, k, halo, v, partly)


def attention_rest(info, q, k, v, block, partly=None):
    rows, width = q.shape

    def at(offset):
        return pl.BlockSpec(
            (WINDOW, width), lambda i, s: (jnp.where(s[1] == block, i, 0) + offset, 0)
        )

    def body(info_ref, q_ref, kp_ref, kc_ref, vp_ref, vc_ref, *rest):
        @pl.when(info_ref[1] == block)
        def _():
            attention_body(False, info_ref, q_ref, kp_ref, kc_ref, vp_ref, vc_ref, rest[-1])

        if partly is not None:

            @pl.when(info_ref[1] != block)
            def _():
                rest[-1][...] = rest[0][...]

    kept = [] if partly is None else [partly]
    return pl.pallas_call(
        body,
        out_shape=jax.ShapeDtypeStruct((rows, width), F32),
        grid_spec=pltpu.PrefetchScalarGridSpec(
            num_scalar_prefetch=1,
            grid=(rows // WINDOW - 1,),
            in_specs=[at(1), at(0), at(1), at(0), at(1)]
            + [pl.BlockSpec((WINDOW, width), lambda i, s: (1, 0)) for _ in kept],
            out_specs=at(1),
        ),
        input_output_aliases={6: 0} if kept else {},
        compiler_params=params(),
        name=f"attention_rest_{block}",
    )(info, q, k, k, v, v, *kept)


SLOTS = 8
RING = 4


class Chunk:
    def __init__(self, name, spans):
        self.name = name
        self.spans = spans
        self.span = sum(n for _, _, n in spans)
        self.rows = SLOTS * self.span


EARLY = Chunk("early", ((0, 0, 40), (1, 0, 8)))
LATE = Chunk("late", ((1, 8, 32),))
CHUNKS = (EARLY, LATE)
UNITS = EARLY.rows + LATE.rows


def factors(gate_pre, up_pre, back, rate_ref, x_ref, at):
    rate = rate_ref[:, at]
    back = back * rate
    sig = 0.5 * jnp.tanh(0.5 * gate_pre) + 0.5
    active = gate_pre * sig
    x_ref[0, :, at] = (back * up_pre * (sig + active * (1.0 - sig))).astype(BF16)
    x_ref[1, :, at] = (back * active).astype(BF16)
    x_ref[2, :, at] = (active * up_pre * rate).astype(BF16)


def tile_factors(w_ref, keys_ref, values_ref, rate_ref, x_ref, at):
    keys = keys_ref[at]
    factors(
        dot(w_ref[0], keys, NT),
        dot(w_ref[1], keys, NT),
        dot(w_ref[2], values_ref[at], NT),
        rate_ref,
        x_ref,
        at,
    )


TILE = 512


class Tokens:
    def __init__(self, key_hbm, value_hbm, keys_ref, values_ref, sems):
        self.pairs = ((key_hbm, keys_ref), (value_hbm, values_ref))
        self.sems = sems
        self.count = keys_ref.shape[0] // TILE

    def at(self, t):
        return pl.ds(pl.multiple_of(t * TILE, TILE), TILE)

    def copies(self, t):
        return [
            pltpu.make_async_copy(hbm.at[self.at(t)], ref.at[self.at(t)], self.sems.at[n, t])
            for n, (hbm, ref) in enumerate(self.pairs)
        ]

    def start(self, t):
        for copy in self.copies(t):
            copy.start()

    def wait(self, t):
        for copy in self.copies(t):
            copy.wait()


def contract(x_ref, keys_ref, values_ref, outs):
    for m in range(3):
        right = (values_ref if m == 2 else keys_ref)[...]
        term = dot(x_ref[m], right, NN)
        base = 0
        for chunk, (mine_ref, theirs_ref) in zip(CHUNKS, outs):
            span = chunk.span
            for d in range(RING):
                for e, ref in enumerate((mine_ref, theirs_ref)):
                    at = base + span * (2 * d + e)
                    ref[d, m * span : (m + 1) * span] = term[at : at + span].astype(BF16)
            base += chunk.rows


def order_rows(info_ref, raw_ref, w_ref, m):
    half = raw_ref.shape[1] // 2
    owned = half // SLOTS
    z, c = info_ref[2], info_ref[3]
    base = 0
    for chunk in CHUNKS:
        for d in range(RING):
            for e in range(2):
                owner = 2 * lax.rem(z + d, RING) + (c if e == 0 else 1 - c)
                rows = [
                    raw_ref[m, pl.ds(pl.multiple_of(owner * owned + h * half + lo, 8), n)]
                    for h, lo, n in chunk.spans
                ]
                w_ref[m, base : base + chunk.span] = jnp.concatenate(rows, 0).astype(BF16)
                base += chunk.span


def fill_gathered(sources, w_ref):
    base, at = 0, 0
    for chunk in CHUNKS:
        for d in range(RING):
            for e in range(2):
                from_there = (-d) % RING
                ref = sources[RING].at[from_there] if e else sources[from_there]
                for m in range(3):
                    here = at + m * chunk.span
                    w_ref[m, base : base + chunk.span] = ref[here : here + chunk.span]
                base += chunk.span
        at += 3 * chunk.span


HERE = pl.BlockSpec(memory_space=pltpu.VMEM)
ANYWHERE = pl.BlockSpec(memory_space=pl.ANY)


SPLIT = 3 * EARLY.span
PIECE = SPLIT + 3 * LATE.span


def fetch(info, sources, height):
    rows, width = sources[0].shape

    def body(info_ref, *refs):
        ins, o_ref, sems = refs[: len(sources)], refs[-2], refs[-1]
        copies = [
            pltpu.make_async_copy(
                i.at[pl.ds(rows - height, height)], o_ref.at[n], sems.at[n]
            )
            for n, i in enumerate(ins)
        ]
        for copy in copies:
            copy.start()
        for copy in copies:
            copy.wait()

    return pl.pallas_call(
        body,
        out_shape=jax.ShapeDtypeStruct((len(sources), height, width), BF16),
        grid_spec=pltpu.PrefetchScalarGridSpec(
            num_scalar_prefetch=1,
            grid=(1,),
            in_specs=[ANYWHERE] * len(sources),
            out_specs=HERE,
            scratch_shapes=[pltpu.SemaphoreType.DMA((len(sources),))],
        ),
        compiler_params=params(16),
        name="fetch",
    )(info, *sources)


def piece_shapes(width, chunked):
    heights = (SPLIT, PIECE - SPLIT) if chunked else (PIECE,)
    return [
        jax.ShapeDtypeStruct((RING, height, width), BF16) for height in heights for _ in range(2)
    ]


def gradient_first(info, initial, keys, values, rates):
    rows, width = keys.shape

    def body(info_ref, raw_ref, key_hbm, value_hbm, rate_ref, mine, theirs, w_out, *refs):
        w_ref, x_ref, ks_ref, vs_ref, save_sem, t_sems = refs

        @pl.when(info_ref[1] == 0)
        def _():
            tokens = Tokens(key_hbm, value_hbm, ks_ref, vs_ref, t_sems)
            save = pltpu.make_async_copy(w_ref, w_out, save_sem)
            first_keys, first_values = tokens.copies(0)
            first_keys.start()
            first_values.start()
            tokens.start(1)
            pre = []
            at = pl.ds(0, TILE)
            for m in range(3):
                order_rows(info_ref, raw_ref, w_ref, m)
                if m == 0:
                    first_keys.wait()
                if m == 2:
                    first_values.wait()
                pre.append(dot(w_ref[m], (vs_ref if m == 2 else ks_ref)[at], NT))
            factors(*pre, rate_ref, x_ref, at)

            def one_tile(t, carry):
                @pl.when(t + 1 < tokens.count)
                def _():
                    tokens.start(t + 1)

                tokens.wait(t)
                tile_factors(w_ref, ks_ref, vs_ref, rate_ref, x_ref, tokens.at(t))
                return carry

            lax.fori_loop(1, tokens.count, one_tile, 0)
            save.start()
            halves = [
                [ref.at[:, at] for ref in (mine, theirs)]
                for at in (slice(0, SPLIT), slice(SPLIT, PIECE))
            ]
            contract(x_ref, ks_ref, vs_ref, halves)
            save.wait()

    return pl.pallas_call(
        body,
        out_shape=piece_shapes(width, False) + [jax.ShapeDtypeStruct((3, UNITS, width), BF16)],
        grid_spec=pltpu.PrefetchScalarGridSpec(
            num_scalar_prefetch=1,
            grid=(1,),
            in_specs=[HERE] + [ANYWHERE] * 2 + [pl.BlockSpec(rates.shape, lambda i, s: (0, 0))],
            out_specs=[HERE] * 2 + [ANYWHERE],
            scratch_shapes=[
                pltpu.VMEM((3, UNITS, width), BF16),
                pltpu.VMEM((3, UNITS, rows), BF16),
                pltpu.VMEM((rows, width), BF16),
                pltpu.VMEM((rows, width), BF16),
                pltpu.SemaphoreType.DMA(()),
                pltpu.SemaphoreType.DMA((2, rows // TILE)),
            ],
        ),
        compiler_params=params(),
        name="gradient_first",
    )(info, initial, keys, values, rates)


def gradient_second(info, gathered, staged, rates, kept):
    _, rows, width = staged.shape
    count = RING + 1

    def body(info_ref, *refs):
        sources, refs = refs[:count], refs[count:]
        staged_ref, rate_ref, _, ma, ta, mb, tb, w_out, w_ref, x_ref, save_sem = refs
        keys_ref, values_ref = staged_ref.at[0], staged_ref.at[1]

        @pl.when(info_ref[1] == 1)
        def _():
            fill_gathered(sources, w_ref)
            save = pltpu.make_async_copy(w_ref, w_out, save_sem)

            def one_tile(t, carry):
                at = pl.ds(pl.multiple_of(t * TILE, TILE), TILE)
                tile_factors(w_ref, keys_ref, values_ref, rate_ref, x_ref, at)
                return carry

            lax.fori_loop(0, rows // TILE, one_tile, 0)
            save.start()
            contract(x_ref, keys_ref, values_ref, ((ma, ta), (mb, tb)))
            save.wait()

    return pl.pallas_call(
        body,
        out_shape=piece_shapes(width, True) + [jax.ShapeDtypeStruct(kept.shape, BF16)],
        grid_spec=pltpu.PrefetchScalarGridSpec(
            num_scalar_prefetch=1,
            grid=(1,),
            in_specs=[HERE] * (count + 1)
            + [pl.BlockSpec(rates.shape, lambda i, s: (0, 0)), ANYWHERE],
            out_specs=[HERE] * 4 + [ANYWHERE],
            scratch_shapes=[
                pltpu.VMEM((3, UNITS, width), BF16),
                pltpu.VMEM((3, UNITS, rows), BF16),
                pltpu.SemaphoreType.DMA(()),
            ],
        ),
        input_output_aliases={count + 3: 4},
        compiler_params=params(30),
        name="gradient_second",
    )(info, *gathered, staged, rates, kept)


def fast_apply(info, queries, weights, gain, attended, tile=512):
    rows, width = queries.shape
    stream = pl.BlockSpec((tile, width), lambda i, s: (i, 0))

    def body(info_ref, q_ref, w_ref, gain_ref, att_ref, o_ref):
        q = q_ref[...]
        gate_pre = dot(q, w_ref[0], NT)
        up_pre = dot(q, w_ref[1], NT)
        sig = 0.5 * jnp.tanh(0.5 * gate_pre) + 0.5
        out = dot((gate_pre * sig * up_pre).astype(BF16), w_ref[2], NN)
        inverse_rms = lax.rsqrt(jnp.mean(out * out, axis=-1, keepdims=True) + EPSILON)
        o_ref[...] = (att_ref[...] + out * inverse_rms * gain_ref[...]).astype(BF16)

    return pl.pallas_call(
        body,
        out_shape=jax.ShapeDtypeStruct((rows, width), BF16),
        grid_spec=pltpu.PrefetchScalarGridSpec(
            num_scalar_prefetch=1,
            grid=(rows // tile,),
            in_specs=[
                stream,
                pl.BlockSpec(
                    weights.shape, lambda i, s: (0, 0, 0), pipeline_mode=pl.Buffered(1)
                ),
                pl.BlockSpec((1, width), lambda i, s: (0, 0)),
                stream,
            ],
            out_specs=stream,
        ),
        compiler_params=params(32),
        name="fast_apply",
    )(info, queries, weights, gain, attended)


def renormalize(previous, gradient):
    moved = previous + gradient
    size = jnp.mean(previous * previous, axis=-1, keepdims=True) + EPSILON
    moved_size = jnp.mean(moved * moved, axis=-1, keepdims=True) + EPSILON
    return moved * (jnp.sqrt(size) / jnp.sqrt(moved_size))


def total(mine_ref, other_ref, *arrived):
    out = mine_ref[0].astype(F32) + other_ref[0].astype(F32)
    for ref in arrived:
        out = out + ref[...].astype(F32)
    return out


def middle_call(info, mine, other, arrived, fast_weights):
    _, height, width = mine.shape
    owned = fast_weights.shape[1] // (2 * SLOTS)

    def half(h):
        return pl.BlockSpec(
            (3, owned, width), lambda i, s: (0, h * SLOTS + 2 * s[2] + s[3], 0)
        )

    def body(info_ref, mine_ref, other_ref, a_ref, b_ref, c_ref, w0_ref, w1_ref, cast_ref, keep_ref):
        gradient = total(mine_ref, other_ref, a_ref, b_ref, c_ref)
        base = 0
        for chunk in CHUNKS:
            for m in range(3):
                old = [(w0_ref, w1_ref)[h][m, lo : lo + n] for h, lo, n in chunk.spans]
                here = slice(base, base + chunk.span)
                new = renormalize(jnp.concatenate(old, 0), gradient[here])
                cast_ref[here] = new.astype(BF16)
                if chunk is EARLY:
                    keep_ref[m] = new[:owned]
                base += chunk.span

    return pl.pallas_call(
        body,
        out_shape=(
            jax.ShapeDtypeStruct((height, width), BF16),
            jax.ShapeDtypeStruct((3, owned, width), F32),
        ),
        grid_spec=pltpu.PrefetchScalarGridSpec(
            num_scalar_prefetch=1,
            grid=(1,),
            in_specs=[HERE] * 5 + [half(0), half(1)],
            out_specs=[HERE] * 2,
        ),
        compiler_params=params(16),
        name="middle_rows",
    )(info, mine, other, *arrived, fast_weights, fast_weights)


def sum_body(mine_ref, other_ref, a_ref, b_ref, both_ref, near_ref, far_ref):
    gradient = total(mine_ref, other_ref, a_ref, b_ref, both_ref.at[:SPLIT])
    owned, rest = near_ref.shape[1], far_ref.shape[1]
    for m in range(3):
        at = m * (owned + rest)
        near_ref[m] = gradient[at : at + owned].astype(BF16)
        far_ref[m] = gradient[at + owned : at + owned + rest]


def sum_call(mine, other, arrived):
    _, span3, width = mine.shape
    owned = EARLY.spans[0][2]
    return pl.pallas_call(
        sum_body,
        out_shape=(
            jax.ShapeDtypeStruct((3, owned, width), BF16),
            jax.ShapeDtypeStruct((3, span3 // 3 - owned, width), F32),
        ),
        in_specs=[HERE] * 5,
        out_specs=[HERE] * 2,
        compiler_params=pltpu.CompilerParams(vmem_limit_bytes=16 << 20),
        name="second_sum",
    )(mine, other, *arrived)


def final_far(info, mine, other, arrived, cast, far):
    shape = (3, EARLY.spans[0][2], cast.shape[1])

    def body(info_ref, mine_ref, other_ref, a_ref, b_ref, both_ref, cast_ref, far_ref, o_ref):
        rest = far_ref.shape[1]
        owned = EARLY.span - rest

        @pl.when(info_ref[1] == 1)
        def _():
            gradient = total(mine_ref, other_ref, a_ref, b_ref, both_ref.at[SPLIT:])
            for m in range(3):
                at = m * EARLY.span
                early = cast_ref[at : at + EARLY.span].astype(F32)[owned:]
                o_ref[m, :rest] = renormalize(early, far_ref[m])
                at = m * LATE.span
                late = cast_ref[SPLIT + at : SPLIT + at + LATE.span].astype(F32)
                o_ref[m, rest:] = renormalize(late, gradient[at : at + LATE.span])

    return pl.pallas_call(
        body,
        out_shape=jax.ShapeDtypeStruct(shape, F32),
        grid_spec=pltpu.PrefetchScalarGridSpec(
            num_scalar_prefetch=1, grid=(1,), in_specs=[HERE] * 7, out_specs=HERE
        ),
        cost_estimate=pl.CostEstimate(
            flops=40_000_000_000, bytes_accessed=100_000_000, transcendentals=0
        ),
        compiler_params=params(16),
        name="final_far",
    )(info, mine, other, *arrived, cast, far)


def final_near(info, middle, near, far_rows):
    def body(info_ref, middle_ref, near_ref, far_ref, o_ref):
        @pl.when(info_ref[1] == 0)
        def _():
            for m in range(3):
                o_ref[m] = renormalize(middle_ref[m], near_ref[m].astype(F32))

        @pl.when(info_ref[1] == 1)
        def _():
            o_ref[...] = far_ref[...]

    return pl.pallas_call(
        body,
        out_shape=jax.ShapeDtypeStruct(middle.shape, F32),
        grid_spec=pltpu.PrefetchScalarGridSpec(
            num_scalar_prefetch=1, grid=(1,), in_specs=[HERE] * 3, out_specs=HERE
        ),
        compiler_params=params(16),
        name="final_near",
    )(info, middle, near, far_rows)


def send(x, pairs):
    return lax.ppermute(x, "seq", pairs)


def along_z(d):
    return [
        (8 * b + 2 * z + c, 8 * b + 2 * ((z + d) % RING) + c)
        for b in range(2)
        for z in range(RING)
        for c in range(2)
    ]


SIBLING = [(k, k ^ 1) for k in range(16)]
ACROSS = [(k, k + 8) for k in range(8)]
BACK = [(k + 8, k) for k in range(8)]


def in_hbm(x):
    return pltpu.with_memory_space_constraint(x, pltpu.HBM)


def after(x, *others):
    return lax.optimization_barrier((x, *others))[0]


def joined(mine, other):
    return [
        (mine[d].astype(F32) + other[d].astype(F32)).astype(BF16) for d in range(1, RING)
    ]


def around(pieces):
    return [send(piece, along_z(d + 1)) for d, piece in enumerate(pieces)]


def shards(
    attn_query, attn_key, attn_value, fast_query, fast_key, fast_value, rates, fast_weights, gain
):
    row_count, width = attn_query.shape
    seq = lax.axis_index("seq").astype(jnp.int32)
    info = jnp.stack([seq, seq // 8, (seq % 8) // 2, seq % 2])
    initial = jnp.transpose(fast_weights[0], (1, 0, 2))
    tokens = (in_hbm(fast_key), in_hbm(fast_value), in_hbm(rates.reshape(1, row_count)))
    attn = tuple(in_hbm(x) for x in (attn_query, attn_key, attn_value))

    onward = [(i, (i + 1) % 16) for i in range(16)]
    tails = fetch(info, attn[1:], WINDOW)

    mine, theirs, weights = gradient_first(after(info, tails), initial, *tokens)
    halo = send(tails, onward)
    other = send(theirs, SIBLING)
    parts = joined(after(mine, halo), other)
    ring = around(parts)
    attended = attention_rest(after(info, *parts), *attn, 1)
    cast, middle = middle_call(after(info, attended), mine, other, ring, initial)
    own = send(cast, ACROSS)
    attended = attention_rest(after(info, cast), *attn, 0, attended)

    staged = fetch(after(info, attended), tokens[:2], row_count)
    own = after(own, staged)
    ring = around([own] * (RING - 1))
    attended = attention_first(after(info, own, staged), *attn, halo, attended)
    column = [own] + [after(piece, attended) for piece in ring]
    beside = send(jnp.stack(column), SIBLING)
    mine_a, theirs_a, mine_b, theirs_b, weights = gradient_second(
        info, [*column, beside], staged, tokens[2], weights
    )
    other_a = send(theirs_a, SIBLING)
    other_b = send(theirs_b, SIBLING)
    part_a = joined(mine_a, other_a)
    part_b = joined(mine_b, other_b)
    both = jnp.concatenate([part_a[1], part_b[1]], 0)
    ring_a = [send(part_a[0], along_z(1)), send(part_a[2], along_z(3))]
    ring_b = [send(part_b[0], along_z(1)), send(part_b[2], along_z(3))]
    both = send(both, along_z(2))
    mixed = fast_apply(after(info, *part_a, *part_b), fast_query, weights, gain, attended)
    near, far = sum_call(after(mine_a, mixed), other_a, [*ring_a, both])
    near = send(near, BACK)
    far_rows = final_far(after(info, far), mine_b, other_b, [*ring_b, both], own, far)
    final = final_near(info, middle, near, far_rows)
    return mixed, jnp.transpose(final, (1, 0, 2))[None]


def solution(mesh):
    in_specs = (
        P("seq", "head"),
        P("seq", "head"),
        P("seq", "head"),
        P("seq", "head"),
        P("seq", "head"),
        P("seq", "head"),
        P("seq", "head"),
        P("head", None, None, None),
        P("head", None),
    )
    out_specs = (P("seq", "head"), P("head", "seq", None, None))
    return jax.shard_map(shards, mesh=mesh, in_specs=in_specs, out_specs=out_specs, check_vma=False)
```

```python
import math
from functools import partial

import jax
import jax.numpy as jnp
from jax import lax
from jax.experimental import pallas as pl
from jax.experimental.pallas import tpu as pltpu
from jax.sharding import PartitionSpec as P

AH = 128
WINDOW = 512
SUB = 256
EPSILON = 1e-06
F32 = jnp.float32
BF16 = jnp.bfloat16


def dot(a, b, contract):
    return lax.dot_general(a, b, (contract, ((), ())), preferred_element_type=F32)


NT = ((1,), (1,))
NN = ((1,), (0,))


def params(mib=40):
    return pltpu.CompilerParams(
        dimension_semantics=("arbitrary",), vmem_limit_bytes=mib << 20
    )


def attention_body(first, info_ref, q_ref, kp_ref, kc_ref, vp_ref, vc_ref, o_ref):
    heads = q_ref.shape[1] // AH
    scale = math.log2(math.e) / math.sqrt(AH)
    row = lax.broadcasted_iota(jnp.int32, (SUB, SUB), 0)
    col = lax.broadcasted_iota(jnp.int32, (SUB, SUB), 1)
    older = col > row
    ones = jnp.ones((SUB, AH), BF16)
    bias = jnp.where(info_ref[0] == 0, -1e30, 0.0).astype(F32) if first else None
    for h in range(heads):
        cols = slice(h * AH, (h + 1) * AH)
        keys = [kp_ref[:SUB, cols], kp_ref[SUB:, cols], kc_ref[:SUB, cols], kc_ref[SUB:, cols]]
        values = [
            jnp.concatenate([v, ones], 1)
            for v in (vp_ref[:SUB, cols], vp_ref[SUB:, cols], vc_ref[:SUB, cols], vc_ref[SUB:, cols])
        ]
        for strip in range(2):
            q = q_ref[strip * SUB : (strip + 1) * SUB, cols]
            old, mid, new = (dot(q, keys[strip + n], NT) for n in range(3))
            if first:
                old = old + bias
                if strip == 0:
                    mid = mid + bias
            edge = jnp.where(older, old, new)
            top = jnp.max(jnp.maximum(edge, mid), axis=1, keepdims=True)
            edge = jnp.exp2((edge - top) * scale)
            mid = jnp.exp2((mid - top) * scale).astype(BF16)
            old = jnp.where(older, edge, 0.0).astype(BF16)
            new = jnp.where(older, 0.0, edge).astype(BF16)
            out = (
                dot(old, values[strip], NN)
                + dot(mid, values[strip + 1], NN)
                + dot(new, values[strip + 2], NN)
            )
            o_ref[strip * SUB : (strip + 1) * SUB, cols] = out[:, :AH] / out[:, AH:]


def attention_first(info, q, k, v, halo, partly):
    rows, width = q.shape
    tile = pl.BlockSpec((WINDOW, width), lambda i, s: (0, 0))

    def past(n):
        return pl.BlockSpec((None, WINDOW, width), lambda i, s: (n, 0, 0))

    def body(info_ref, q_ref, kp_ref, kc_ref, vp_ref, vc_ref, _, o_ref):
        attention_body(True, info_ref, q_ref, kp_ref, kc_ref, vp_ref, vc_ref, o_ref)

    return pl.pallas_call(
        body,
        out_shape=jax.ShapeDtypeStruct((rows, width), F32),
        grid_spec=pltpu.PrefetchScalarGridSpec(
            num_scalar_prefetch=1,
            grid=(1,),
            in_specs=[tile, past(0), tile, past(1), tile, pl.BlockSpec(memory_space=pl.ANY)],
            out_specs=tile,
        ),
        input_output_aliases={6: 0},
        compiler_params=params(),
        name="attention_first",
    )(info, q, halo, k, halo, v, partly)


def attention_rest(info, q, k, v, block, partly=None):
    rows, width = q.shape

    def at(offset):
        return pl.BlockSpec(
            (WINDOW, width), lambda i, s: (jnp.where(s[1] == block, i, 0) + offset, 0)
        )

    def body(info_ref, q_ref, kp_ref, kc_ref, vp_ref, vc_ref, *rest):
        @pl.when(info_ref[1] == block)
        def _():
            attention_body(False, info_ref, q_ref, kp_ref, kc_ref, vp_ref, vc_ref, rest[-1])

        if partly is not None:

            @pl.when(info_ref[1] != block)
            def _():
                rest[-1][...] = rest[0][...]

    kept = [] if partly is None else [partly]
    return pl.pallas_call(
        body,
        out_shape=jax.ShapeDtypeStruct((rows, width), F32),
        grid_spec=pltpu.PrefetchScalarGridSpec(
            num_scalar_prefetch=1,
            grid=(rows // WINDOW - 1,),
            in_specs=[at(1), at(0), at(1), at(0), at(1)]
            + [pl.BlockSpec((WINDOW, width), lambda i, s: (1, 0)) for _ in kept],
            out_specs=at(1),
        ),
        input_output_aliases={6: 0} if kept else {},
        compiler_params=params(),
        name=f"attention_rest_{block}",
    )(info, q, k, k, v, v, *kept)


SLOTS = 8
RING = 4


class Chunk:
    def __init__(self, name, spans):
        self.name = name
        self.spans = spans
        self.span = sum(n for _, _, n in spans)
        self.rows = SLOTS * self.span


EARLY = Chunk("early", ((0, 0, 40), (1, 0, 8)))
LATE = Chunk("late", ((1, 8, 32),))
CHUNKS = (EARLY, LATE)
OWNED = EARLY.span + LATE.span
UNITS = RING * OWNED


def factors(gate_pre, up_pre, back, rate_ref, x_ref, at):
    rate = rate_ref[:, at]
    back = back * rate
    sig = 0.5 * jnp.tanh(0.5 * gate_pre) + 0.5
    active = gate_pre * sig
    x_ref[0, :, at] = (back * up_pre * (sig + active * (1.0 - sig))).astype(BF16)
    x_ref[1, :, at] = (back * active).astype(BF16)
    x_ref[2, :, at] = (active * up_pre * rate).astype(BF16)


def tile_factors(w_ref, keys_ref, values_ref, rate_ref, x_ref, at):
    keys = keys_ref[at]
    factors(
        dot(w_ref[0], keys, NT),
        dot(w_ref[1], keys, NT),
        dot(w_ref[2], values_ref[at], NT),
        rate_ref,
        x_ref,
        at,
    )


TILE = 512


class Tokens:
    def __init__(self, key_hbm, value_hbm, keys_ref, values_ref, sems):
        self.pairs = ((key_hbm, keys_ref), (value_hbm, values_ref))
        self.sems = sems
        self.count = keys_ref.shape[0] // TILE

    def at(self, t):
        return pl.ds(pl.multiple_of(t * TILE, TILE), TILE)

    def copies(self, t):
        return [
            pltpu.make_async_copy(hbm.at[self.at(t)], ref.at[self.at(t)], self.sems.at[n, t])
            for n, (hbm, ref) in enumerate(self.pairs)
        ]

    def start(self, t):
        for copy in self.copies(t):
            copy.start()

    def wait(self, t):
        for copy in self.copies(t):
            copy.wait()


def piece_rows():
    at = 0
    for chunk, lo in zip(CHUNKS, (0, EARLY.span)):
        for m in range(3):
            yield m, lo, at + m * chunk.span, chunk.span
        at += 3 * chunk.span


def contract(x_ref, keys_ref, values_ref, out_ref):
    for m in range(3):
        term = dot(x_ref[m], (values_ref if m == 2 else keys_ref)[...], NN)
        for d in range(RING):
            for matrix, lo, at, n in piece_rows():
                if matrix == m:
                    here = d * OWNED + lo
                    out_ref[d, at : at + n] = term[here : here + n].astype(BF16)


def order_rows(info_ref, raw_ref, w_ref, m, other):
    half = raw_ref.shape[1] // 2
    owned = half // SLOTS
    z, c = info_ref[2], info_ref[3]
    for d in range(RING):
        owner = 2 * lax.rem(z + d, RING) + (1 - c if other else c)
        first = pl.multiple_of(owner * owned, 8)
        rows = [raw_ref[m, pl.ds(first, owned)], raw_ref[m, pl.ds(first + half, owned)]]
        w_ref[m, d * OWNED : (d + 1) * OWNED] = jnp.concatenate(rows, 0).astype(BF16)


def fill_gathered(sources, w_ref):
    for d in range(RING):
        for m, lo, at, n in piece_rows():
            here = d * OWNED + lo
            w_ref[m, here : here + n] = sources[(-d) % RING][at : at + n]


HERE = pl.BlockSpec(memory_space=pltpu.VMEM)
ANYWHERE = pl.BlockSpec(memory_space=pl.ANY)


SPLIT = 3 * EARLY.span
PIECE = SPLIT + 3 * LATE.span


def fetch(info, sources, height):
    rows, width = sources[0].shape

    def body(info_ref, *refs):
        ins, o_ref, sems = refs[: len(sources)], refs[-2], refs[-1]
        copies = [
            pltpu.make_async_copy(
                i.at[pl.ds(rows - height, height)], o_ref.at[n], sems.at[n]
            )
            for n, i in enumerate(ins)
        ]
        for copy in copies:
            copy.start()
        for copy in copies:
            copy.wait()

    return pl.pallas_call(
        body,
        out_shape=jax.ShapeDtypeStruct((len(sources), height, width), BF16),
        grid_spec=pltpu.PrefetchScalarGridSpec(
            num_scalar_prefetch=1,
            grid=(1,),
            in_specs=[ANYWHERE] * len(sources),
            out_specs=HERE,
            scratch_shapes=[pltpu.SemaphoreType.DMA((len(sources),))],
        ),
        compiler_params=params(16),
        name="fetch",
    )(info, *sources)


def gradient_call(name, block, other, fill, info, sources, staged, rates, kept=None, tokens=()):
    width = sources[0].shape[-1]
    rows = rates.shape[1]
    first = len(tokens) > 0
    count = len(sources)
    extra = [] if kept is None else [kept]
    held = list(tokens) if first else [staged]
    row0 = UNITS if other else 0

    def body(info_ref, *refs):
        source_refs, refs = refs[:count], refs[count:]
        held_refs, refs = refs[: len(held)], refs[len(held) :]
        rate_ref, refs = refs[0], refs[1 + len(extra) :]
        out_ref, w_out, *refs = refs
        if first:
            staged_ref, w_ref, x_ref, save_sem, t_sems = refs
        else:
            staged_ref = held_refs[0]
            w_ref, x_ref, save_sem = refs
        keys_ref, values_ref = staged_ref.at[0], staged_ref.at[1]
        save = pltpu.make_async_copy(w_ref, w_out.at[:, pl.ds(row0, UNITS)], save_sem)
        steps = rows // TILE
        if first:
            arriving = Tokens(*held_refs, keys_ref, values_ref, t_sems)

            @pl.when(info_ref[1] != block)
            def _():
                for t in range(steps):
                    arriving.start(t)
                for t in range(steps):
                    arriving.wait(t)

        @pl.when(info_ref[1] == block)
        def _():
            if first:
                arriving.start(0)
            fill(info_ref, source_refs, w_ref)

            def one_tile(t, carry):
                if first:

                    @pl.when(t + 1 < steps)
                    def _():
                        arriving.start(t + 1)

                    arriving.wait(t)
                at = pl.ds(pl.multiple_of(t * TILE, TILE), TILE)
                tile_factors(w_ref, keys_ref, values_ref, rate_ref, x_ref, at)
                return carry

            lax.fori_loop(0, steps, one_tile, 0)
            save.start()
            contract(x_ref, keys_ref, values_ref, out_ref)
            save.wait()

    shapes = [
        jax.ShapeDtypeStruct((RING, PIECE, width), BF16),
        jax.ShapeDtypeStruct((3, 2 * UNITS, width), BF16),
    ]
    scratch = [
        pltpu.VMEM((3, UNITS, width), BF16),
        pltpu.VMEM((3, UNITS, rows), BF16),
        pltpu.SemaphoreType.DMA(()),
    ]
    if first:
        shapes.append(jax.ShapeDtypeStruct((2, rows, width), BF16))
        scratch.append(pltpu.SemaphoreType.DMA((2, rows // TILE)))
    return pl.pallas_call(
        body,
        out_shape=shapes,
        grid_spec=pltpu.PrefetchScalarGridSpec(
            num_scalar_prefetch=1,
            grid=(1,),
            in_specs=[HERE] * count
            + [ANYWHERE if first else HERE] * len(held)
            + [pl.BlockSpec(rates.shape, lambda i, s: (0, 0))]
            + [ANYWHERE] * len(extra),
            out_specs=[HERE, ANYWHERE] + [HERE] * (len(shapes) - 2),
            scratch_shapes=scratch,
        ),
        input_output_aliases={count + len(held) + 2: 1} if extra else {},
        compiler_params=params(30),
        name=name,
    )(info, *sources, *held, rates, *extra)


def fill_initial(other):
    def fill(info_ref, source_refs, w_ref):
        for m in range(3):
            order_rows(info_ref, source_refs[0], w_ref, m, other)

    return fill


def fill_column(info_ref, source_refs, w_ref):
    fill_gathered(source_refs, w_ref)


def fill_beside(info_ref, source_refs, w_ref):
    fill_gathered([source_refs[0].at[d] for d in range(RING)], w_ref)


def fast_apply(info, queries, weights, gain, attended, tile=512):
    rows, width = queries.shape
    stream = pl.BlockSpec((tile, width), lambda i, s: (i, 0))

    def body(info_ref, q_ref, w_ref, gain_ref, att_ref, o_ref):
        q = q_ref[...]
        gate_pre = dot(q, w_ref[0], NT)
        up_pre = dot(q, w_ref[1], NT)
        sig = 0.5 * jnp.tanh(0.5 * gate_pre) + 0.5
        out = dot((gate_pre * sig * up_pre).astype(BF16), w_ref[2], NN)
        inverse_rms = lax.rsqrt(jnp.mean(out * out, axis=-1, keepdims=True) + EPSILON)
        o_ref[...] = (att_ref[...] + out * inverse_rms * gain_ref[...]).astype(BF16)

    return pl.pallas_call(
        body,
        out_shape=jax.ShapeDtypeStruct((rows, width), BF16),
        grid_spec=pltpu.PrefetchScalarGridSpec(
            num_scalar_prefetch=1,
            grid=(rows // tile,),
            in_specs=[
                stream,
                pl.BlockSpec(
                    weights.shape, lambda i, s: (0, 0, 0), pipeline_mode=pl.Buffered(1)
                ),
                pl.BlockSpec((1, width), lambda i, s: (0, 0)),
                stream,
            ],
            out_specs=stream,
        ),
        compiler_params=params(32),
        name="fast_apply",
    )(info, queries, weights, gain, attended)


def renormalize(previous, gradient):
    moved = previous + gradient
    size = jnp.mean(previous * previous, axis=-1, keepdims=True) + EPSILON
    moved_size = jnp.mean(moved * moved, axis=-1, keepdims=True) + EPSILON
    return moved * (jnp.sqrt(size) / jnp.sqrt(moved_size))


def total(mine_ref, other_ref, at, *arrived):
    out = mine_ref[0, at].astype(F32) + other_ref[0, at].astype(F32)
    for ref in arrived:
        out = out + ref[...].astype(F32)
    return out


def middle_call(info, mine, other, arrived, fast_weights):
    _, height, width = mine.shape
    owned = fast_weights.shape[1] // (2 * SLOTS)

    def half(h):
        return pl.BlockSpec(
            (3, owned, width), lambda i, s: (0, h * SLOTS + 2 * s[2] + s[3], 0)
        )

    def body(info_ref, mine_ref, other_ref, a_ref, b_ref, c_ref, w0_ref, w1_ref, cast_ref, keep_ref):
        gradient = total(mine_ref, other_ref, slice(0, PIECE), a_ref, b_ref, c_ref)
        base = 0
        for chunk in CHUNKS:
            for m in range(3):
                old = [(w0_ref, w1_ref)[h][m, lo : lo + n] for h, lo, n in chunk.spans]
                here = slice(base, base + chunk.span)
                new = renormalize(jnp.concatenate(old, 0), gradient[here])
                cast_ref[here] = new.astype(BF16)
                if chunk is EARLY:
                    keep_ref[m] = new[:owned]
                base += chunk.span

    return pl.pallas_call(
        body,
        out_shape=(
            jax.ShapeDtypeStruct((height, width), BF16),
            jax.ShapeDtypeStruct((3, owned, width), F32),
        ),
        grid_spec=pltpu.PrefetchScalarGridSpec(
            num_scalar_prefetch=1,
            grid=(1,),
            in_specs=[HERE] * 5 + [half(0), half(1)],
            out_specs=[HERE] * 2,
        ),
        compiler_params=params(16),
        name="middle_rows",
    )(info, mine, other, *arrived, fast_weights, fast_weights)


def sum_body(mine_ref, other_ref, a_ref, b_ref, both_ref, near_ref, far_ref):
    gradient = total(mine_ref, other_ref, slice(0, SPLIT), a_ref, b_ref, both_ref.at[:SPLIT])
    owned, rest = near_ref.shape[1], far_ref.shape[1]
    for m in range(3):
        at = m * (owned + rest)
        near_ref[m] = gradient[at : at + owned].astype(BF16)
        far_ref[m] = gradient[at + owned : at + owned + rest]


def sum_call(mine, other, arrived):
    width = mine.shape[2]
    owned = EARLY.spans[0][2]
    return pl.pallas_call(
        sum_body,
        out_shape=(
            jax.ShapeDtypeStruct((3, owned, width), BF16),
            jax.ShapeDtypeStruct((3, EARLY.span - owned, width), F32),
        ),
        in_specs=[HERE] * 5,
        out_specs=[HERE] * 2,
        compiler_params=pltpu.CompilerParams(vmem_limit_bytes=16 << 20),
        name="second_sum",
    )(mine, other, *arrived)


def final_far(info, mine, other, arrived, cast, far):
    shape = (3, EARLY.spans[0][2], cast.shape[2])

    def body(info_ref, mine_ref, other_ref, a_ref, b_ref, both_ref, cast_ref, far_ref, o_ref):
        rest = far_ref.shape[1]
        owned = EARLY.span - rest

        @pl.when(info_ref[1] == 1)
        def _():
            late = slice(SPLIT, PIECE)
            gradient = total(mine_ref, other_ref, late, a_ref, b_ref, both_ref.at[SPLIT:])
            for m in range(3):
                at = m * EARLY.span
                early = cast_ref[0, at : at + EARLY.span].astype(F32)[owned:]
                o_ref[m, :rest] = renormalize(early, far_ref[m])
                at = m * LATE.span
                old = cast_ref[0, SPLIT + at : SPLIT + at + LATE.span].astype(F32)
                o_ref[m, rest:] = renormalize(old, gradient[at : at + LATE.span])

    return pl.pallas_call(
        body,
        out_shape=jax.ShapeDtypeStruct(shape, F32),
        grid_spec=pltpu.PrefetchScalarGridSpec(
            num_scalar_prefetch=1, grid=(1,), in_specs=[HERE] * 7, out_specs=HERE
        ),
        cost_estimate=pl.CostEstimate(
            flops=40_000_000_000, bytes_accessed=100_000_000, transcendentals=0
        ),
        compiler_params=params(16),
        name="final_far",
    )(info, mine, other, *arrived, cast, far)


def final_near(info, middle, near, far_rows):
    def body(info_ref, middle_ref, near_ref, far_ref, o_ref):
        @pl.when(info_ref[1] == 0)
        def _():
            for m in range(3):
                o_ref[m] = renormalize(middle_ref[m], near_ref[m].astype(F32))

        @pl.when(info_ref[1] == 1)
        def _():
            o_ref[...] = far_ref[...]

    return pl.pallas_call(
        body,
        out_shape=jax.ShapeDtypeStruct(middle.shape, F32),
        grid_spec=pltpu.PrefetchScalarGridSpec(
            num_scalar_prefetch=1, grid=(1,), in_specs=[HERE] * 3, out_specs=HERE
        ),
        compiler_params=params(16),
        name="final_near",
    )(info, middle, near, far_rows)


def send(x, pairs):
    return lax.ppermute(x, "seq", pairs)


def along_z(d):
    return [
        (8 * b + 2 * z + c, 8 * b + 2 * ((z + d) % RING) + c)
        for b in range(2)
        for z in range(RING)
        for c in range(2)
    ]


SIBLING = [(k, k ^ 1) for k in range(16)]
ACROSS = [(k, (k ^ 1) + 8) for k in range(8)]
BACK = [(k + 8, k) for k in range(8)]


def in_hbm(x):
    return pltpu.with_memory_space_constraint(x, pltpu.HBM)


def after(x, *others):
    return lax.optimization_barrier((x, *others))[0]


def joined(mine, other, at=slice(0, PIECE), places=range(1, RING)):
    return [(mine[d, at].astype(F32) + other[d, at].astype(F32)).astype(BF16) for d in places]


def around(pieces):
    return [send(piece, along_z(d + 1)) for d, piece in enumerate(pieces)]


def shards(
    attn_query, attn_key, attn_value, fast_query, fast_key, fast_value, rates, fast_weights, gain
):
    row_count, width = attn_query.shape
    seq = lax.axis_index("seq").astype(jnp.int32)
    info = jnp.stack([seq, seq // 8, (seq % 8) // 2, seq % 2])
    initial = jnp.transpose(fast_weights[0], (1, 0, 2))
    tokens = (in_hbm(fast_key), in_hbm(fast_value), in_hbm(rates.reshape(1, row_count)))
    attn = tuple(in_hbm(x) for x in (attn_query, attn_key, attn_value))

    onward = [(i, (i + 1) % 16) for i in range(16)]
    tails = fetch(info, attn[1:], WINDOW)

    theirs, weights, staged = gradient_call(
        "first_theirs", 0, True, fill_initial(True), after(info, tails), [initial], None,
        tokens[2], tokens=tokens[:2],
    )
    halo = send(tails, onward)
    other = send(theirs, SIBLING)
    mine, weights = gradient_call(
        "first_mine", 0, False, fill_initial(False), after(info, theirs), [initial], staged,
        tokens[2], weights,
    )
    parts = joined(after(mine, halo), other)
    ring = around(parts)
    attended = attention_rest(after(info, *parts), *attn, 1)
    cast, middle = middle_call(after(info, attended), mine, other, ring, initial)
    own = send(cast, ACROSS)
    attended = attention_rest(after(info, cast), *attn, 0, attended)

    own = after(own, attended)
    ring = around([own] * (RING - 1))
    attended = attention_first(after(info, own), *attn, halo, attended)
    column = [own] + [after(piece, attended) for piece in ring]
    beside = send(jnp.stack(column), SIBLING)
    theirs, weights = gradient_call(
        "second_theirs", 1, True, fill_column, info, column, staged, tokens[2], weights
    )
    other = send(theirs, SIBLING)
    mine, weights = gradient_call(
        "second_mine", 1, False, fill_beside, after(info, theirs), [beside], staged, tokens[2],
        weights,
    )
    early, late = slice(0, SPLIT), slice(SPLIT, PIECE)
    part_a = joined(mine, other, early, (1, 3))
    part_b = joined(mine, other, late, (1, 3))
    (both,) = joined(mine, other, places=(2,))
    ring_a = [send(part, along_z(d)) for part, d in zip(part_a, (1, 3))]
    ring_b = [send(part, along_z(d)) for part, d in zip(part_b, (1, 3))]
    both_there = send(both, along_z(2))
    ready = after(info, both, *part_a, *part_b)
    mixed = fast_apply(ready, fast_query, weights, gain, attended)
    near, far = sum_call(after(mine, mixed), other, [*ring_a, both_there])
    near = send(near, BACK)
    far_rows = final_far(after(info, far), mine, other, [*ring_b, both_there], beside, far)
    final = final_near(info, middle, near, far_rows)
    return mixed, jnp.transpose(final, (1, 0, 2))[None]


def solution(mesh):
    in_specs = (
        P("seq", "head"),
        P("seq", "head"),
        P("seq", "head"),
        P("seq", "head"),
        P("seq", "head"),
        P("seq", "head"),
        P("seq", "head"),
        P("head", None, None, None),
        P("head", None),
    )
    out_specs = (P("seq", "head"), P("head", "seq", None, None))
    return jax.shard_map(shards, mesh=mesh, in_specs=in_specs, out_specs=out_specs, check_vma=False)
```

```python
import math
from functools import partial

import jax
import jax.numpy as jnp
from jax import lax
from jax.experimental import pallas as pl
from jax.experimental.pallas import tpu as pltpu
from jax.sharding import PartitionSpec as P

AH = 128
WINDOW = 512
SUB = 256
EPSILON = 1e-06
F32 = jnp.float32
BF16 = jnp.bfloat16


def dot(a, b, contract):
    return lax.dot_general(a, b, (contract, ((), ())), preferred_element_type=F32)


NT = ((1,), (1,))
NN = ((1,), (0,))


def params(mib=40):
    return pltpu.CompilerParams(
        dimension_semantics=("arbitrary",), vmem_limit_bytes=mib << 20
    )


def attention_body(first, info_ref, q_ref, kp_ref, kc_ref, vp_ref, vc_ref, o_ref):
    heads = q_ref.shape[1] // AH
    scale = math.log2(math.e) / math.sqrt(AH)
    row = lax.broadcasted_iota(jnp.int32, (SUB, SUB), 0)
    col = lax.broadcasted_iota(jnp.int32, (SUB, SUB), 1)
    older = col > row
    ones = jnp.ones((SUB, AH), BF16)
    bias = jnp.where(info_ref[0] == 0, -1e30, 0.0).astype(F32) if first else None
    for h in range(heads):
        cols = slice(h * AH, (h + 1) * AH)
        keys = [kp_ref[:SUB, cols], kp_ref[SUB:, cols], kc_ref[:SUB, cols], kc_ref[SUB:, cols]]
        values = [
            jnp.concatenate([v, ones], 1)
            for v in (vp_ref[:SUB, cols], vp_ref[SUB:, cols], vc_ref[:SUB, cols], vc_ref[SUB:, cols])
        ]
        for strip in range(2):
            q = q_ref[strip * SUB : (strip + 1) * SUB, cols]
            old, mid, new = (dot(q, keys[strip + n], NT) for n in range(3))
            if first:
                old = old + bias
                if strip == 0:
                    mid = mid + bias
            edge = jnp.where(older, old, new)
            top = jnp.max(jnp.maximum(edge, mid), axis=1, keepdims=True)
            edge = jnp.exp2((edge - top) * scale)
            mid = jnp.exp2((mid - top) * scale).astype(BF16)
            old = jnp.where(older, edge, 0.0).astype(BF16)
            new = jnp.where(older, 0.0, edge).astype(BF16)
            out = (
                dot(old, values[strip], NN)
                + dot(mid, values[strip + 1], NN)
                + dot(new, values[strip + 2], NN)
            )
            o_ref[strip * SUB : (strip + 1) * SUB, cols] = out[:, :AH] / out[:, AH:]


def attention_first(info, q, k, v, halo, partly):
    rows, width = q.shape
    tile = pl.BlockSpec((WINDOW, width), lambda i, s: (0, 0))

    def past(n):
        return pl.BlockSpec((None, WINDOW, width), lambda i, s: (n, 0, 0))

    def body(info_ref, q_ref, kp_ref, kc_ref, vp_ref, vc_ref, _, o_ref):
        attention_body(True, info_ref, q_ref, kp_ref, kc_ref, vp_ref, vc_ref, o_ref)

    return pl.pallas_call(
        body,
        out_shape=jax.ShapeDtypeStruct((rows, width), F32),
        grid_spec=pltpu.PrefetchScalarGridSpec(
            num_scalar_prefetch=1,
            grid=(1,),
            in_specs=[tile, past(0), tile, past(1), tile, pl.BlockSpec(memory_space=pl.ANY)],
            out_specs=tile,
        ),
        input_output_aliases={6: 0},
        compiler_params=params(),
        name="attention_first",
    )(info, q, halo, k, halo, v, partly)


def attention_rest(info, q, k, v, block, partly=None):
    rows, width = q.shape

    def at(offset):
        return pl.BlockSpec(
            (WINDOW, width), lambda i, s: (jnp.where(s[1] == block, i, 0) + offset, 0)
        )

    def body(info_ref, q_ref, kp_ref, kc_ref, vp_ref, vc_ref, *rest):
        @pl.when(info_ref[1] == block)
        def _():
            attention_body(False, info_ref, q_ref, kp_ref, kc_ref, vp_ref, vc_ref, rest[-1])

        if partly is not None:

            @pl.when(info_ref[1] != block)
            def _():
                rest[-1][...] = rest[0][...]

    kept = [] if partly is None else [partly]
    return pl.pallas_call(
        body,
        out_shape=jax.ShapeDtypeStruct((rows, width), F32),
        grid_spec=pltpu.PrefetchScalarGridSpec(
            num_scalar_prefetch=1,
            grid=(rows // WINDOW - 1,),
            in_specs=[at(1), at(0), at(1), at(0), at(1)]
            + [pl.BlockSpec((WINDOW, width), lambda i, s: (1, 0)) for _ in kept],
            out_specs=at(1),
        ),
        input_output_aliases={6: 0} if kept else {},
        compiler_params=params(),
        name=f"attention_rest_{block}",
    )(info, q, k, k, v, v, *kept)


SLOTS = 8
RING = 4


class Chunk:
    def __init__(self, name, spans):
        self.name = name
        self.spans = spans
        self.span = sum(n for _, _, n in spans)
        self.rows = SLOTS * self.span


EARLY = Chunk("early", ((0, 0, 40), (1, 0, 8)))
LATE = Chunk("late", ((1, 8, 32),))
CHUNKS = (EARLY, LATE)
OWNED = EARLY.span + LATE.span
UNITS = RING * OWNED


def factors(gate_pre, up_pre, back, rate_ref, x_ref, at):
    rate = rate_ref[:, at]
    back = back * rate
    sig = 0.5 * jnp.tanh(0.5 * gate_pre) + 0.5
    active = gate_pre * sig
    x_ref[0, :, at] = (back * up_pre * (sig + active * (1.0 - sig))).astype(BF16)
    x_ref[1, :, at] = (back * active).astype(BF16)
    x_ref[2, :, at] = (active * up_pre * rate).astype(BF16)


def tile_factors(w_ref, keys_ref, values_ref, rate_ref, x_ref, at):
    keys = keys_ref[at]
    factors(
        dot(w_ref[0], keys, NT),
        dot(w_ref[1], keys, NT),
        dot(w_ref[2], values_ref[at], NT),
        rate_ref,
        x_ref,
        at,
    )


TILE = 512


class Tokens:
    def __init__(self, key_hbm, value_hbm, keys_ref, values_ref, sems):
        self.pairs = ((key_hbm, keys_ref), (value_hbm, values_ref))
        self.sems = sems
        self.count = keys_ref.shape[0] // TILE

    def at(self, t):
        return pl.ds(pl.multiple_of(t * TILE, TILE), TILE)

    def copies(self, t):
        return [
            pltpu.make_async_copy(hbm.at[self.at(t)], ref.at[self.at(t)], self.sems.at[n, t])
            for n, (hbm, ref) in enumerate(self.pairs)
        ]

    def start(self, t):
        for copy in self.copies(t):
            copy.start()

    def wait(self, t):
        for copy in self.copies(t):
            copy.wait()


def piece_rows():
    at = 0
    for chunk, lo in zip(CHUNKS, (0, EARLY.span)):
        for m in range(3):
            yield m, lo, at + m * chunk.span, chunk.span
        at += 3 * chunk.span


def contract(x_ref, keys_ref, values_ref, out_ref):
    for m in range(3):
        term = dot(x_ref[m], (values_ref if m == 2 else keys_ref)[...], NN)
        for d in range(RING):
            for matrix, lo, at, n in piece_rows():
                if matrix == m:
                    here = d * OWNED + lo
                    out_ref[d, at : at + n] = term[here : here + n].astype(BF16)


def order_rows(info_ref, raw_ref, w_ref, m, other):
    half = raw_ref.shape[1] // 2
    owned = half // SLOTS
    z, c = info_ref[2], info_ref[3]
    for d in range(RING):
        owner = 2 * lax.rem(z + d, RING) + (1 - c if other else c)
        first = pl.multiple_of(owner * owned, 8)
        rows = [raw_ref[m, pl.ds(first, owned)], raw_ref[m, pl.ds(first + half, owned)]]
        w_ref[m, d * OWNED : (d + 1) * OWNED] = jnp.concatenate(rows, 0).astype(BF16)


def fill_gathered(sources, w_ref):
    for d in range(RING):
        for m, lo, at, n in piece_rows():
            here = d * OWNED + lo
            w_ref[m, here : here + n] = sources[(-d) % RING][at : at + n]


HERE = pl.BlockSpec(memory_space=pltpu.VMEM)
ANYWHERE = pl.BlockSpec(memory_space=pl.ANY)


SPLIT = 3 * EARLY.span
PIECE = SPLIT + 3 * LATE.span


def fetch(info, sources, height):
    rows, width = sources[0].shape

    def body(info_ref, *refs):
        ins, o_ref, sems = refs[: len(sources)], refs[-2], refs[-1]
        copies = [
            pltpu.make_async_copy(
                i.at[pl.ds(rows - height, height)], o_ref.at[n], sems.at[n]
            )
            for n, i in enumerate(ins)
        ]
        for copy in copies:
            copy.start()
        for copy in copies:
            copy.wait()

    return pl.pallas_call(
        body,
        out_shape=jax.ShapeDtypeStruct((len(sources), height, width), BF16),
        grid_spec=pltpu.PrefetchScalarGridSpec(
            num_scalar_prefetch=1,
            grid=(1,),
            in_specs=[ANYWHERE] * len(sources),
            out_specs=HERE,
            scratch_shapes=[pltpu.SemaphoreType.DMA((len(sources),))],
        ),
        compiler_params=params(16),
        name="fetch",
    )(info, *sources)


def gradient_call(name, block, other, fill, info, sources, staged, rates, kept=None, tokens=()):
    width = sources[0].shape[-1]
    rows = rates.shape[1]
    first = len(tokens) > 0
    count = len(sources)
    extra = [] if kept is None else [kept]
    held = list(tokens) if first else [staged]
    row0 = UNITS if other else 0

    def body(info_ref, *refs):
        source_refs, refs = refs[:count], refs[count:]
        held_refs, refs = refs[: len(held)], refs[len(held) :]
        rate_ref, refs = refs[0], refs[1 + len(extra) :]
        out_ref, w_out, *refs = refs
        if first:
            staged_ref, w_ref, x_ref, save_sem, t_sems = refs
        else:
            staged_ref = held_refs[0]
            w_ref, x_ref, save_sem = refs
        keys_ref, values_ref = staged_ref.at[0], staged_ref.at[1]
        save = pltpu.make_async_copy(w_ref, w_out.at[:, pl.ds(row0, UNITS)], save_sem)
        steps = rows // TILE
        if first:
            arriving = Tokens(*held_refs, keys_ref, values_ref, t_sems)

            @pl.when(info_ref[1] != block)
            def _():
                for t in range(steps):
                    arriving.start(t)
                for t in range(steps):
                    arriving.wait(t)

        @pl.when(info_ref[1] == block)
        def _():
            if first:
                arriving.start(0)
            fill(info_ref, source_refs, w_ref)

            def one_tile(t, carry):
                if first:

                    @pl.when(t + 1 < steps)
                    def _():
                        arriving.start(t + 1)

                    arriving.wait(t)
                at = pl.ds(pl.multiple_of(t * TILE, TILE), TILE)
                tile_factors(w_ref, keys_ref, values_ref, rate_ref, x_ref, at)
                return carry

            lax.fori_loop(0, steps, one_tile, 0)
            save.start()
            contract(x_ref, keys_ref, values_ref, out_ref)
            save.wait()

    shapes = [
        jax.ShapeDtypeStruct((RING, PIECE, width), BF16),
        jax.ShapeDtypeStruct((3, 2 * UNITS, width), BF16),
    ]
    scratch = [
        pltpu.VMEM((3, UNITS, width), BF16),
        pltpu.VMEM((3, UNITS, rows), BF16),
        pltpu.SemaphoreType.DMA(()),
    ]
    if first:
        shapes.append(jax.ShapeDtypeStruct((2, rows, width), BF16))
        scratch.append(pltpu.SemaphoreType.DMA((2, rows // TILE)))
    return pl.pallas_call(
        body,
        out_shape=shapes,
        grid_spec=pltpu.PrefetchScalarGridSpec(
            num_scalar_prefetch=1,
            grid=(1,),
            in_specs=[HERE] * count
            + [ANYWHERE if first else HERE] * len(held)
            + [pl.BlockSpec(rates.shape, lambda i, s: (0, 0))]
            + [ANYWHERE] * len(extra),
            out_specs=[HERE, ANYWHERE] + [HERE] * (len(shapes) - 2),
            scratch_shapes=scratch,
        ),
        input_output_aliases={count + len(held) + 2: 1} if extra else {},
        compiler_params=params(30),
        name=name,
    )(info, *sources, *held, rates, *extra)


def fill_initial(other):
    def fill(info_ref, source_refs, w_ref):
        for m in range(3):
            order_rows(info_ref, source_refs[0], w_ref, m, other)

    return fill


def fill_column(info_ref, source_refs, w_ref):
    fill_gathered(source_refs, w_ref)


def fill_beside(info_ref, source_refs, w_ref):
    fill_gathered([source_refs[0].at[d] for d in range(RING)], w_ref)


def fast_apply(info, queries, weights, gain, attended, tiles, partly=None, tile=512):
    rows, width = queries.shape
    stream = pl.BlockSpec((tile, width), lambda i, s: (i + tiles[0], 0))
    kept = [] if partly is None else [partly]

    def body(info_ref, q_ref, w_ref, gain_ref, att_ref, *rest):
        q = q_ref[...]
        gate_pre = dot(q, w_ref[0], NT)
        up_pre = dot(q, w_ref[1], NT)
        sig = 0.5 * jnp.tanh(0.5 * gate_pre) + 0.5
        out = dot((gate_pre * sig * up_pre).astype(BF16), w_ref[2], NN)
        inverse_rms = lax.rsqrt(jnp.mean(out * out, axis=-1, keepdims=True) + EPSILON)
        rest[-1][...] = (att_ref[...] + out * inverse_rms * gain_ref[...]).astype(BF16)

    return pl.pallas_call(
        body,
        out_shape=jax.ShapeDtypeStruct((rows, width), BF16),
        grid_spec=pltpu.PrefetchScalarGridSpec(
            num_scalar_prefetch=1,
            grid=(tiles[1] - tiles[0],),
            in_specs=[
                stream,
                pl.BlockSpec(
                    weights.shape, lambda i, s: (0, 0, 0), pipeline_mode=pl.Buffered(1)
                ),
                pl.BlockSpec((1, width), lambda i, s: (0, 0)),
                stream,
            ]
            + [ANYWHERE for _ in kept],
            out_specs=stream,
        ),
        input_output_aliases={5: 0} if kept else {},
        cost_estimate=pl.CostEstimate(
            flops=1_380_000_000, bytes_accessed=0, transcendentals=0
        ),
        compiler_params=params(32),
        name=f"fast_apply_{tiles[0]}",
    )(info, queries, weights, gain, attended, *kept)


def renormalize(previous, gradient):
    moved = previous + gradient
    size = jnp.mean(previous * previous, axis=-1, keepdims=True) + EPSILON
    moved_size = jnp.mean(moved * moved, axis=-1, keepdims=True) + EPSILON
    return moved * (jnp.sqrt(size) / jnp.sqrt(moved_size))


def total(mine_ref, other_ref, at, *arrived):
    out = mine_ref[0, at].astype(F32) + other_ref[0, at].astype(F32)
    for ref in arrived:
        out = out + ref[...].astype(F32)
    return out


def middle_call(info, mine, other, arrived, fast_weights):
    _, height, width = mine.shape
    owned = fast_weights.shape[1] // (2 * SLOTS)

    def half(h):
        return pl.BlockSpec(
            (3, owned, width), lambda i, s: (0, h * SLOTS + 2 * s[2] + s[3], 0)
        )

    def body(info_ref, mine_ref, other_ref, a_ref, b_ref, c_ref, w0_ref, w1_ref, cast_ref, keep_ref):
        gradient = total(mine_ref, other_ref, slice(0, PIECE), a_ref, b_ref, c_ref)
        base = 0
        for chunk in CHUNKS:
            for m in range(3):
                old = [(w0_ref, w1_ref)[h][m, lo : lo + n] for h, lo, n in chunk.spans]
                here = slice(base, base + chunk.span)
                new = renormalize(jnp.concatenate(old, 0), gradient[here])
                cast_ref[here] = new.astype(BF16)
                if chunk is EARLY:
                    keep_ref[m] = new[:owned]
                base += chunk.span

    return pl.pallas_call(
        body,
        out_shape=(
            jax.ShapeDtypeStruct((height, width), BF16),
            jax.ShapeDtypeStruct((3, owned, width), F32),
        ),
        grid_spec=pltpu.PrefetchScalarGridSpec(
            num_scalar_prefetch=1,
            grid=(1,),
            in_specs=[HERE] * 5 + [half(0), half(1)],
            out_specs=[HERE] * 2,
        ),
        compiler_params=params(16),
        name="middle_rows",
    )(info, mine, other, *arrived, fast_weights, fast_weights)


def sum_body(mine_ref, other_ref, a_ref, b_ref, both_ref, near_ref, far_ref):
    gradient = total(mine_ref, other_ref, slice(0, SPLIT), a_ref, b_ref, both_ref.at[:SPLIT])
    owned, rest = near_ref.shape[1], far_ref.shape[1]
    for m in range(3):
        at = m * (owned + rest)
        near_ref[m] = gradient[at : at + owned].astype(BF16)
        far_ref[m] = gradient[at + owned : at + owned + rest]


def sum_call(mine, other, arrived):
    width = mine.shape[2]
    owned = EARLY.spans[0][2]
    return pl.pallas_call(
        sum_body,
        out_shape=(
            jax.ShapeDtypeStruct((3, owned, width), BF16),
            jax.ShapeDtypeStruct((3, EARLY.span - owned, width), F32),
        ),
        in_specs=[HERE] * 5,
        out_specs=[HERE] * 2,
        compiler_params=pltpu.CompilerParams(vmem_limit_bytes=16 << 20),
        name="second_sum",
    )(mine, other, *arrived)


def final_far(info, mine, other, arrived, cast, far):
    shape = (3, EARLY.spans[0][2], cast.shape[2])

    def body(info_ref, mine_ref, other_ref, a_ref, b_ref, both_ref, cast_ref, far_ref, o_ref):
        rest = far_ref.shape[1]
        owned = EARLY.span - rest

        @pl.when(info_ref[1] == 1)
        def _():
            late = slice(SPLIT, PIECE)
            gradient = total(mine_ref, other_ref, late, a_ref, b_ref, both_ref.at[SPLIT:])
            for m in range(3):
                at = m * EARLY.span
                early = cast_ref[0, at : at + EARLY.span].astype(F32)[owned:]
                o_ref[m, :rest] = renormalize(early, far_ref[m])
                at = m * LATE.span
                old = cast_ref[0, SPLIT + at : SPLIT + at + LATE.span].astype(F32)
                o_ref[m, rest:] = renormalize(old, gradient[at : at + LATE.span])

    return pl.pallas_call(
        body,
        out_shape=jax.ShapeDtypeStruct(shape, F32),
        grid_spec=pltpu.PrefetchScalarGridSpec(
            num_scalar_prefetch=1, grid=(1,), in_specs=[HERE] * 7, out_specs=HERE
        ),
        cost_estimate=pl.CostEstimate(
            flops=920_000_000, bytes_accessed=0, transcendentals=0
        ),
        compiler_params=params(16),
        name="final_far",
    )(info, mine, other, *arrived, cast, far)


def final_near(info, middle, near, far_rows):
    def body(info_ref, middle_ref, near_ref, far_ref, o_ref):
        @pl.when(info_ref[1] == 0)
        def _():
            for m in range(3):
                o_ref[m] = renormalize(middle_ref[m], near_ref[m].astype(F32))

        @pl.when(info_ref[1] == 1)
        def _():
            o_ref[...] = far_ref[...]

    return pl.pallas_call(
        body,
        out_shape=jax.ShapeDtypeStruct(middle.shape, F32),
        grid_spec=pltpu.PrefetchScalarGridSpec(
            num_scalar_prefetch=1, grid=(1,), in_specs=[HERE] * 3, out_specs=HERE
        ),
        compiler_params=params(16),
        name="final_near",
    )(info, middle, near, far_rows)


def send(x, pairs):
    return lax.ppermute(x, "seq", pairs)


def along_z(d):
    return [
        (8 * b + 2 * z + c, 8 * b + 2 * ((z + d) % RING) + c)
        for b in range(2)
        for z in range(RING)
        for c in range(2)
    ]


SIBLING = [(k, k ^ 1) for k in range(16)]
ACROSS = [(k, (k ^ 1) + 8) for k in range(8)]
BACK = [(k + 8, k) for k in range(8)]


def in_hbm(x):
    return pltpu.with_memory_space_constraint(x, pltpu.HBM)


def after(x, *others):
    return lax.optimization_barrier((x, *others))[0]


def joined(mine, other, at=slice(0, PIECE), places=range(1, RING)):
    return [(mine[d, at].astype(F32) + other[d, at].astype(F32)).astype(BF16) for d in places]


def around(pieces):
    return [send(piece, along_z(d + 1)) for d, piece in enumerate(pieces)]


def shards(
    attn_query, attn_key, attn_value, fast_query, fast_key, fast_value, rates, fast_weights, gain
):
    row_count, width = attn_query.shape
    seq = lax.axis_index("seq").astype(jnp.int32)
    info = jnp.stack([seq, seq // 8, (seq % 8) // 2, seq % 2])
    initial = jnp.transpose(fast_weights[0], (1, 0, 2))
    tokens = (in_hbm(fast_key), in_hbm(fast_value), in_hbm(rates.reshape(1, row_count)))
    attn = tuple(in_hbm(x) for x in (attn_query, attn_key, attn_value))

    onward = [(i, (i + 1) % 16) for i in range(16)]
    tails = fetch(info, attn[1:], WINDOW)

    theirs, weights, staged = gradient_call(
        "first_theirs", 0, True, fill_initial(True), after(info, tails), [initial], None,
        tokens[2], tokens=tokens[:2],
    )
    halo = send(tails, onward)
    other = send(theirs, SIBLING)
    mine, weights = gradient_call(
        "first_mine", 0, False, fill_initial(False), after(info, theirs), [initial], staged,
        tokens[2], weights,
    )
    parts = joined(after(mine, halo), other)
    ring = around(parts)
    attended = attention_rest(after(info, *parts), *attn, 1)
    cast, middle = middle_call(after(info, attended), mine, other, ring, initial)
    own = send(cast, ACROSS)
    attended = attention_rest(after(info, cast), *attn, 0, attended)

    own = after(own, attended)
    ring = around([own] * (RING - 1))
    attended = attention_first(after(info, own), *attn, halo, attended)
    column = [own] + [after(piece, attended) for piece in ring]
    beside = send(jnp.stack(column), SIBLING)
    theirs, weights = gradient_call(
        "second_theirs", 1, True, fill_column, info, column, staged, tokens[2], weights
    )
    other = send(theirs, SIBLING)
    mine, weights = gradient_call(
        "second_mine", 1, False, fill_beside, after(info, theirs), [beside], staged, tokens[2],
        weights,
    )
    early, late = slice(0, SPLIT), slice(SPLIT, PIECE)
    part_a = joined(mine, other, early, (1, 3))
    part_b = joined(mine, other, late, (1, 3))
    (both,) = joined(mine, other, places=(2,))
    ring_a = [send(part, along_z(d)) for part, d in zip(part_a, (1, 3))]
    ring_b = [send(part, along_z(d)) for part, d in zip(part_b, (1, 3))]
    both_there = send(both, along_z(2))
    ready = after(info, both, *part_a, *part_b)
    mixed = fast_apply(ready, fast_query, weights, gain, attended, (0, 2))
    near, far = sum_call(after(mine, mixed), other, [*ring_a, both_there])
    near = send(near, BACK)
    mixed = fast_apply(after(info, far), fast_query, weights, gain, attended, (2, 4), mixed)
    far_rows = final_far(after(info, mixed), mine, other, [*ring_b, both_there], beside, far)
    final = final_near(info, middle, near, far_rows)
    return mixed, jnp.transpose(final, (1, 0, 2))[None]


def solution(mesh):
    in_specs = (
        P("seq", "head"),
        P("seq", "head"),
        P("seq", "head"),
        P("seq", "head"),
        P("seq", "head"),
        P("seq", "head"),
        P("seq", "head"),
        P("head", None, None, None),
        P("head", None),
    )
    out_specs = (P("seq", "head"), P("head", "seq", None, None))
    return jax.shard_map(shards, mesh=mesh, in_specs=in_specs, out_specs=out_specs, check_vma=False)
```
